32 devices in a mesh: ctx: 8 (over z, y), shard: 4 (over x, core).
Axes of the slice: x: 2, y: 2, z: 4, core: 2. Of those that a mesh axis runs over, the one named last changes fastest.
Arguments:
- block_in: bfloat16 [1024, 1024], P('ctx'), may hold values from -6 to 6
- attn_gain: float32 [1024], replicated, may hold values from 0.5 to 1.5
- q_weight: bfloat16 [1024, 1024], P(None, 'shard'), may hold values from -0.1875 to 0.1875
- k_weight: bfloat16 [1024, 512], P(None, 'shard'), may hold values from -0.1875 to 0.1875
- v_weight: bfloat16 [1024, 512], P(None, 'shard'), may hold values from -0.1875 to 0.1875
- o_weight: bfloat16 [1024, 1024], P('shard'), may hold values from -1.5 to 1.5
- moe_gain: float32 [1024], replicated, may hold values from 0.5 to 1.5
- router_weight: bfloat16 [1024, 16], replicated, may hold values from -0.1875 to 0.1875
- expert_gate: bfloat16 [16, 1024, 512], P('shard'), may hold values from -0.1875 to 0.1875
- expert_up: bfloat16 [16, 1024, 512], P('shard'), may hold values from -0.1875 to 0.1875
- expert_down: bfloat16 [16, 512, 1024], P('shard'), may hold values from -0.5 to 0.5
- routes: int32 [1024, 8], P('ctx'), may hold values from 0 to 15, all different within a row; in each aligned block of 128 rows (0 to 127, 128 to 255, ...) at most 112 rows name the same one
- out_grad: float32 [1024, 1024], P('ctx'), may hold values from -6 to 6
Outputs:
- block_out: float32 [1024, 1024], P('ctx')
- in_grad: float32 [1024, 1024], P('ctx')
- attn_gain_grad: float32 [1024], P('ctx')
- q_weight_grad: float32 [1024, 1024], P('ctx', 'shard')
- k_weight_grad: float32 [1024, 512], P('ctx', 'shard')
- v_weight_grad: float32 [1024, 512], P('ctx', 'shard')
- o_weight_grad: float32 [1024, 1024], P('shard', 'ctx')
- moe_gain_grad: float32 [1024], P('ctx')
- router_grad: float32 [1024, 16], P('ctx')
- gate_grad: float32 [16, 1024, 512], P('shard', 'ctx')
- up_grad: float32 [16, 1024, 512], P('shard', 'ctx')
- down_grad: float32 [16, 512, 1024], P('shard', None, 'ctx')
The draws below stay inside these ranges and needn't reach their ends.
Inputs may be any that keep to these rules, and one draw needn't show every extreme that they name: `routes`: each row names 8 different experts; in each aligned block of 128 rows (128; a device may hold several) no expert is named by more than 112 rows.
All inputs are finite; a program needn't handle non-finite values.
Results may differ from the reference program's by a relative error of at most 0.015.
Values may be sent and summed in bfloat16 or wider, within the bound.
No kernel may reach another device: no remote copies, remote signals or barrier semaphores. Data moves between devices by JAX's collectives and lax.ppermute only.
A program may use at most 128 MiB of HBM per device.

```python
import math
import jax
import jax.numpy as jnp
import numpy as np
from jax import lax

D = 1024
QH = 16
KVH = 8
HD = 64
FF = 512
TOP = 8
TOK_DEV = 128
EXPERTS = 16
CAP = 112
TOKENS = 1024


def steps_of(own_key, extent, split, least, top_value):
    factor_of = 1.0
    for position, parts in split:
        steps = jax.random.uniform(jax.random.fold_in(jax.random.fold_in(own_key, 6), position), (parts,), jnp.float32, least / len(split), top_value / len(split))
        factor_of = factor_of * jnp.repeat(jnp.exp(steps), extent[position] // parts).reshape((-1,) + (1,) * (len(extent) - 1 - position))
    return factor_of


def routed_block(rng, own, number, rows, number_of, top, most, lean):
    ranking = jax.random.permutation(rng, number_of)
    heavy_load, usual = portions_of(number_of, rows * top, most, lean, True), portions_of(number_of, rows * top, most, lean, False)
    places = jnp.arange(number_of)

    def named(tallies, rotation):
        used = int((tallies > 0).sum())
        fixed = max(1, used // 4)
        shifted = fixed + (places - fixed + rotation * (used - fixed)) % max(1, number_of - fixed)
        return jnp.zeros((number_of,), jnp.int32).at[ranking[jnp.where(places < fixed, places, shifted)]].set(jnp.asarray(tallies, jnp.int32))

    tallies = jnp.where(number % 4 == 0, named(heavy_load, number // 4), named(usual, number - number // 4 - 1))
    mixed = jax.random.permutation(jax.random.fold_in(own, 3), number_of)
    donor, taker = mixed[0:number_of // 2 * 2:2], mixed[1:number_of // 2 * 2:2]
    slack = jnp.minimum(tallies[donor] - 1, most - tallies[taker]) // 2
    slack = jnp.where((donor == ranking[0]) | (taker == ranking[0]) | (tallies[taker] == 0), 0, jnp.maximum(slack, 0))
    shifted = jax.random.randint(jax.random.fold_in(own, 4), (number_of // 2,), 0, 1 << 20) % (slack + 1)
    tallies = tallies.at[donor].add(-shifted).at[taker].add(shifted)
    items = jnp.searchsorted(jnp.cumsum(tallies), jnp.arange(rows * top), side="right").astype(jnp.int32)
    grid = items.reshape(top, rows).T
    grid = grid[jax.random.permutation(jax.random.fold_in(own, 1), rows)]
    rotation = jax.random.randint(jax.random.fold_in(own, 2), (rows, 1), 0, top)
    return jnp.take_along_axis(grid, (jnp.arange(top)[None, :] + rotation) % top, axis=1)


def portions_of(count, total, reach, lean, full):
    portions = [(1 << 20) // math.isqrt(standing ** lean) + 1 for standing in range(1, count + 1)]
    largest = reach if full else min(reach, max(-(-total // count), total * portions[0] // sum(portions)))
    least = 1 if total - largest >= count - 1 else 0
    holding, surplus = [largest] + [least] * (count - 1), total - largest - least * (count - 1)
    while surplus > 0:
        movable = [i for i in range(1, count) if holding[i] < largest] or [i for i in range(1, count) if holding[i] < reach]
        pool, left = sum([portions[i] for i in movable]), surplus
        for i in movable:
            extra = min(reach - holding[i], max(1, left * portions[i] // pool), surplus)
            holding[i] = holding[i] + extra
            surplus = surplus - extra
    return np.array(holding)


def noise(key, extent, width, most, cuts=(), kind=jnp.bfloat16):
    level = steps_of(key, extent, cuts, -0.22, 0.18) if cuts else 1.0
    result = jax.random.normal(key, extent, jnp.float32) * width * level
    return jnp.minimum(jnp.maximum(result, -most), most).astype(kind)


def setup_inputs(seed: int = 0) -> dict:
    key_list = jax.random.split(jax.random.key(seed), 14)
    block_in = noise(key_list[0], (TOKENS, D), 1.0, 6.0, ((0, 8),))
    attn_gain = jnp.clip(1.0 + 0.1 * jax.random.normal(key_list[1], (D,), jnp.float32), 0.5, 1.5)
    q_weight = noise(key_list[2], (D, QH * HD), D ** -0.5, 0.1875, ((1, 4),))
    k_weight = noise(key_list[3], (D, KVH * HD), D ** -0.5, 0.1875, ((1, 4),))
    v_weight = noise(key_list[4], (D, KVH * HD), D ** -0.5, 0.1875, ((1, 4),))
    o_weight = noise(key_list[5], (QH * HD, D), 16 ** -0.5, 1.5, ((0, 4),))
    moe_gain = jnp.clip(1.0 + 0.1 * jax.random.normal(key_list[6], (D,), jnp.float32), 0.5, 1.5)
    router_weight = noise(key_list[7], (D, EXPERTS), D ** -0.5, 0.1875)
    expert_gate = noise(key_list[8], (EXPERTS, D, FF), D ** -0.5, 0.1875, ((0, 4),))
    expert_up = noise(key_list[9], (EXPERTS, D, FF), D ** -0.5, 0.1875, ((0, 4),))
    expert_down = noise(key_list[10], (EXPERTS, FF, D), (FF // 4) ** -0.5, 0.5, ((0, 4),))
    routes_keys = jax.random.split(jax.random.fold_in(key_list[11], 1), TOKENS // TOK_DEV)
    routes_turns = jax.random.permutation(jax.random.fold_in(key_list[11], 3), TOKENS // TOK_DEV)
    routes = jax.vmap(lambda own, number: routed_block(jax.random.fold_in(key_list[11], 2), own, number, TOK_DEV, EXPERTS, TOP, CAP, 2))(routes_keys, routes_turns).reshape((TOKENS, TOP))
    out_grad = noise(key_list[12], (TOKENS, D), 1.0, 6.0, ((0, 8),), jnp.float32)
    return dict(block_in=block_in, attn_gain=attn_gain, q_weight=q_weight, k_weight=k_weight, v_weight=v_weight, o_weight=o_weight, moe_gain=moe_gain, router_weight=router_weight, expert_gate=expert_gate, expert_up=expert_up, expert_down=expert_down, routes=routes, out_grad=out_grad)


NORM_EPS = 1e-06
ROPE_BASE = 10000.0

def rope_tables(positions, head_width):
    half_width = head_width // 2
    freq_steps = jnp.arange(half_width, dtype=jnp.float32) * (2.0 / head_width)
    inv_freq = jnp.exp(-math.log(ROPE_BASE) * freq_steps)
    angles = positions.astype(jnp.float32)[:, None] * inv_freq[None, :]
    cos_tab = jnp.concatenate([jnp.cos(angles), jnp.cos(angles)], axis=1)
    sin_tab = jnp.concatenate([jnp.sin(angles), jnp.sin(angles)], axis=1)
    return (cos_tab, sin_tab)

def rotate_heads(head_vals, cos_tab, sin_tab):
    half_width = head_vals.shape[-1] // 2
    turned = jnp.concatenate([-head_vals[..., half_width:], head_vals[..., :half_width]], axis=-1)
    return head_vals * cos_tab[:, None, :] + turned * sin_tab[:, None, :]

def unrotate_heads(head_grads, cos_tab, sin_tab):
    half_width = head_grads.shape[-1] // 2
    scaled = head_grads * sin_tab[:, None, :]
    back = jnp.concatenate([scaled[..., half_width:], -scaled[..., :half_width]], axis=-1)
    return head_grads * cos_tab[:, None, :] + back

def rms_forward(inputs, gain):
    inverse = lax.rsqrt(lax.optimization_barrier(jnp.mean(inputs * inputs, axis=-1, keepdims=True)) + NORM_EPS)
    return (inputs * inverse * gain, inverse)

def rms_backward(inputs, inverse, gain, grads):
    scaled = grads * gain
    inner = lax.optimization_barrier(jnp.mean(scaled * inputs, axis=-1, keepdims=True))
    d_inputs = inverse * scaled - inputs * inverse * inverse * inverse * inner
    d_gain = lax.optimization_barrier(jnp.sum(grads * inputs * inverse, axis=0))
    return (d_inputs, d_gain)

def slot_tables(routes, n_experts):
    expert_ids = jnp.arange(n_experts, dtype=jnp.int32)
    expert_hits = lax.optimization_barrier(jnp.sum((routes[:, :, None] == expert_ids[None, None, :]).astype(jnp.int32), axis=1)).astype(jnp.int32)
    earlier_hits = (jnp.cumsum(expert_hits, axis=0) - expert_hits).astype(jnp.int32)
    slot_ids = jnp.take_along_axis(earlier_hits, routes, axis=1).astype(jnp.int32)
    return (expert_hits, earlier_hits, slot_ids)

def spread_to_experts(values_tk, routes, n_experts):
    expert_ids = jnp.arange(n_experts, dtype=jnp.int32)
    return lax.optimization_barrier(jnp.sum(jnp.where(routes[:, :, None] == expert_ids[None, None, :], values_tk[:, :, None], 0.0), axis=1))

def slot_rows(expert_hits, earlier_hits, weight_table, first_expert, expert_count, capacity):
    local_hits = lax.dynamic_slice_in_dim(expert_hits, first_expert, expert_count, 1).T
    local_earlier = lax.dynamic_slice_in_dim(earlier_hits, first_expert, expert_count, 1).T
    local_weight = lax.dynamic_slice_in_dim(weight_table, first_expert, expert_count, 1).T
    slot_range = jnp.arange(capacity, dtype=jnp.int32)
    matched = (local_hits[:, None, :] > 0) & (local_earlier[:, None, :] == slot_range[None, :, None])
    row_range = jnp.arange(expert_hits.shape[0], dtype=jnp.int32)
    row_ids = lax.optimization_barrier(jnp.sum(jnp.where(matched, row_range[None, None, :], 0), axis=2)).astype(jnp.int32)
    row_valid = jnp.any(matched, axis=2)
    slot_weight = lax.optimization_barrier(jnp.sum(jnp.where(matched, local_weight[:, None, :], 0.0), axis=2))
    return (row_ids, row_valid, slot_weight)

def round_trip(values):
    return lax.optimization_barrier(values.astype(jnp.bfloat16)).astype(jnp.float32)

def reference(block_in, attn_gain, q_weight, k_weight, v_weight, o_weight, moe_gain, router_weight, expert_gate, expert_up, expert_down, routes, out_grad):
    seq_len = block_in.shape[0]
    group = QH // KVH
    scale = HD ** (-0.5)
    q_block = math.gcd(512, seq_len)
    n_qblocks = seq_len // q_block
    positions = jnp.arange(seq_len, dtype=jnp.int32)
    cos_tab, sin_tab = rope_tables(positions, HD)
    resid_in = block_in.astype(jnp.float32)
    normed_one, inverse_one = rms_forward(resid_in, attn_gain)
    normed_one = normed_one.astype(jnp.bfloat16)
    query_rot = rotate_heads(jnp.dot(normed_one, q_weight, preferred_element_type=jnp.float32).reshape(seq_len, QH, HD), cos_tab, sin_tab).astype(jnp.bfloat16)
    key_rot = rotate_heads(jnp.dot(normed_one, k_weight, preferred_element_type=jnp.float32).reshape(seq_len, KVH, HD), cos_tab, sin_tab).astype(jnp.bfloat16)
    value_proj = jnp.dot(normed_one, v_weight, preferred_element_type=jnp.float32).astype(jnp.bfloat16).reshape(seq_len, KVH, HD)
    keys_f = key_rot.astype(jnp.float32)
    values_f = value_proj.astype(jnp.float32)
    query_blocks = query_rot.reshape(n_qblocks, q_block, KVH, group, HD)
    block_ids = jnp.arange(n_qblocks, dtype=jnp.int32)

    def masked_scores(query_blk, block_id):
        query_pos = block_id * q_block + jnp.arange(q_block, dtype=jnp.int32)
        raw = jnp.einsum('tngd,jnd->ngtj', query_blk.astype(jnp.float32), keys_f) * scale
        allowed = positions[None, :] <= query_pos[:, None]
        return jnp.where(allowed[None, None], raw, -jnp.inf)

    def forward_block(inputs_blk):
        query_blk, block_id = inputs_blk
        scores = masked_scores(query_blk, block_id)
        top = lax.optimization_barrier(jnp.max(scores, axis=-1))
        log_total = top + jnp.log(lax.optimization_barrier(jnp.sum(jnp.exp(scores - top[..., None]), axis=-1)))
        probs = round_trip(jnp.exp(scores - log_total[..., None]))
        heads_blk = jnp.einsum('ngtj,jnd->tngd', probs, values_f)
        return (heads_blk.astype(jnp.bfloat16).reshape(q_block, QH * HD), log_total)
    heads_blocks, log_totals = lax.map(forward_block, (query_blocks, block_ids))
    heads_out = heads_blocks.reshape(seq_len, QH * HD)
    resid_mid = resid_in + jnp.dot(heads_out, o_weight, preferred_element_type=jnp.float32)
    normed_two, inverse_two = rms_forward(resid_mid, moe_gain)
    normed_two = normed_two.astype(jnp.bfloat16)
    logits = jnp.dot(normed_two, router_weight, preferred_element_type=jnp.float32)
    gate = jax.nn.softmax(jnp.take_along_axis(logits, routes, axis=1), axis=-1)
    n_blocks = seq_len // TOK_DEV
    gate_f = expert_gate.astype(jnp.float32)
    up_f = expert_up.astype(jnp.float32)
    down_f = expert_down.astype(jnp.float32)

    def moe_block(carry, inputs_blk):
        grad_gate, grad_up, grad_down = carry
        normed_blk, routes_blk, gate_blk, out_grad_blk = inputs_blk
        expert_hits, earlier_hits, slot_ids = slot_tables(routes_blk, EXPERTS)
        gate_table = spread_to_experts(gate_blk, routes_blk, EXPERTS)
        row_ids, row_valid, slot_weight = slot_rows(expert_hits, earlier_hits, gate_table, 0, EXPERTS, CAP)
        buffer = jnp.where(row_valid[..., None], normed_blk[row_ids], jnp.zeros((), jnp.bfloat16))
        buffer_f = buffer.astype(jnp.float32)
        pre_gate = jnp.einsum('ecd,edf->ecf', buffer_f, gate_f)
        pre_up = jnp.einsum('ecd,edf->ecf', buffer_f, up_f)
        sig_gate = jax.nn.sigmoid(pre_gate)
        hidden = round_trip(pre_gate * sig_gate * pre_up)
        expert_out = jnp.einsum('ecf,efd->ecd', hidden, down_f)
        flat_ids = routes_blk * CAP + slot_ids
        picked = expert_out.reshape(EXPERTS * CAP, -1)[flat_ids]
        moe_blk = lax.optimization_barrier(jnp.sum(gate_blk[..., None] * picked, axis=1))
        d_gate_blk = lax.optimization_barrier(jnp.sum(picked * out_grad_blk[:, None, :], axis=-1))
        d_expert_out = round_trip(jnp.where(row_valid, slot_weight, 0.0)[..., None] * out_grad_blk[row_ids])
        d_hidden = jnp.einsum('ecd,efd->ecf', d_expert_out, down_f)
        grad_down = grad_down + jnp.einsum('ecf,ecd->efd', hidden, d_expert_out)
        d_silu = sig_gate * (1.0 + pre_gate * (1.0 - sig_gate))
        d_pre_gate = round_trip(d_hidden * pre_up * d_silu)
        d_pre_up = round_trip(d_hidden * pre_gate * sig_gate)
        grad_gate = grad_gate + jnp.einsum('ecd,ecf->edf', buffer_f, d_pre_gate)
        grad_up = grad_up + jnp.einsum('ecd,ecf->edf', buffer_f, d_pre_up)
        d_buffer = jnp.einsum('ecf,edf->ecd', d_pre_gate, gate_f) + jnp.einsum('ecf,edf->ecd', d_pre_up, up_f)
        d_normed_blk = lax.optimization_barrier(jnp.sum(d_buffer.reshape(EXPERTS * CAP, -1)[flat_ids], axis=1))
        return ((grad_gate, grad_up, grad_down), (moe_blk, d_gate_blk, d_normed_blk))
    zero_in = jnp.zeros((EXPERTS, D, FF), jnp.float32)
    zero_down = jnp.zeros((EXPERTS, FF, D), jnp.float32)
    moe_inputs = (normed_two.reshape(n_blocks, TOK_DEV, D), routes.reshape(n_blocks, TOK_DEV, TOP), gate.reshape(n_blocks, TOK_DEV, TOP), out_grad.reshape(n_blocks, TOK_DEV, D))
    (gate_grad, up_grad, down_grad), (moe_blocks, d_gate_blocks, d_normed_blocks) = lax.scan(moe_block, (zero_in, zero_in, zero_down), moe_inputs)
    block_out = resid_mid + moe_blocks.reshape(seq_len, D)
    d_gate = d_gate_blocks.reshape(seq_len, TOP)
    d_normed_exp = d_normed_blocks.reshape(seq_len, D)
    d_chosen = gate * (d_gate - lax.optimization_barrier(jnp.sum(gate * d_gate, axis=-1, keepdims=True)))
    d_logits = spread_to_experts(d_chosen, routes, EXPERTS)
    router_f = router_weight.astype(jnp.float32)
    d_normed_two = d_normed_exp + jnp.dot(d_logits, router_f.T, precision=lax.Precision.HIGHEST)
    router_grad = jnp.dot(normed_two.astype(jnp.float32).T, d_logits, precision=lax.Precision.HIGHEST)
    d_resid_norm, moe_gain_grad = rms_backward(resid_mid, inverse_two, moe_gain, d_normed_two)
    d_resid_mid = out_grad + d_resid_norm
    d_mid_b = d_resid_mid.astype(jnp.bfloat16)
    o_weight_grad = jnp.dot(heads_out.T, d_mid_b, preferred_element_type=jnp.float32)
    d_heads = jnp.dot(d_mid_b, o_weight.T, preferred_element_type=jnp.float32).astype(jnp.bfloat16)
    d_head_blocks = d_heads.reshape(n_qblocks, q_block, KVH, group, HD)
    out_blocks = heads_blocks.reshape(n_qblocks, q_block, KVH, group, HD)

    def backward_block(carry, inputs_blk):
        d_keys, d_values = carry
        query_blk, out_blk, d_head_blk, log_total, block_id = inputs_blk
        scores = masked_scores(query_blk, block_id)
        probs = jnp.exp(scores - log_total[..., None])
        d_head_f = d_head_blk.astype(jnp.float32)
        delta = lax.optimization_barrier(jnp.sum(d_head_f * out_blk.astype(jnp.float32), axis=-1)).transpose(1, 2, 0)
        d_probs = jnp.einsum('tngd,jnd->ngtj', d_head_f, values_f)
        d_scores = round_trip(probs * (d_probs - delta[..., None]))
        d_query_blk = scale * jnp.einsum('ngtj,jnd->tngd', d_scores, keys_f)
        d_keys = d_keys + scale * jnp.einsum('ngtj,tngd->jnd', d_scores, query_blk.astype(jnp.float32))
        d_values = d_values + jnp.einsum('ngtj,tngd->jnd', round_trip(probs), d_head_f)
        return ((d_keys, d_values), d_query_blk)
    zero_kv = jnp.zeros((seq_len, KVH, HD), jnp.float32)
    (d_keys, d_values), d_query_blocks = lax.scan(backward_block, (zero_kv, zero_kv), (query_blocks, out_blocks, d_head_blocks, log_totals, block_ids))
    d_query = unrotate_heads(d_query_blocks.reshape(seq_len, QH, HD), cos_tab, sin_tab).astype(jnp.bfloat16).reshape(seq_len, QH * HD)
    d_key = unrotate_heads(d_keys, cos_tab, sin_tab).astype(jnp.bfloat16).reshape(seq_len, KVH * HD)
    d_value = d_values.astype(jnp.bfloat16).reshape(seq_len, KVH * HD)
    q_weight_grad = jnp.dot(normed_one.T, d_query, preferred_element_type=jnp.float32)
    k_weight_grad = jnp.dot(normed_one.T, d_key, preferred_element_type=jnp.float32)
    v_weight_grad = jnp.dot(normed_one.T, d_value, preferred_element_type=jnp.float32)
    d_normed_one = jnp.dot(d_query, q_weight.T, preferred_element_type=jnp.float32) + jnp.dot(d_key, k_weight.T, preferred_element_type=jnp.float32) + jnp.dot(d_value, v_weight.T, preferred_element_type=jnp.float32)
    d_resid_first, attn_gain_grad = rms_backward(resid_in, inverse_one, attn_gain, d_normed_one)
    in_grad = d_resid_mid + d_resid_first
    return (block_out, in_grad, attn_gain_grad, q_weight_grad, k_weight_grad, v_weight_grad, o_weight_grad, moe_gain_grad, router_grad, gate_grad, up_grad, down_grad)
```

```python
import functools
import math

import jax
import jax.numpy as jnp
import numpy as np
from jax import lax
from jax.experimental import pallas as pl
from jax.experimental.pallas import tpu as pltpu
from jax.sharding import PartitionSpec as P

HD = 64
NORM_EPS = 1e-06
ROPE_BASE = 10000.0
BF = jnp.bfloat16
F32 = jnp.float32
LANES = 128
COST = 0.05
VMEM_LIMIT = 56 * 1024 * 1024


def nn(a, b):
    return lax.dot_general(a, b, (((1,), (0,)), ((), ())), preferred_element_type=F32)


def nt(a, b):
    return lax.dot_general(a, b, (((1,), (1,)), ((), ())), preferred_element_type=F32)


def tn(a, b):
    return lax.dot_general(a, b, (((0,), (0,)), ((), ())), preferred_element_type=F32)


def rope_constants(seq_len):
    half = HD // 2
    steps = np.arange(half, dtype=np.float32) * np.float32(2.0 / HD)
    inv_freq = np.exp(np.float32(-math.log(ROPE_BASE)) * steps).astype(np.float32)
    angles = np.arange(seq_len, dtype=np.float32)[:, None] * inv_freq[None, :]
    cos, sin = np.cos(angles), np.sin(angles)
    cos_tab = np.concatenate([cos, cos, cos, cos], axis=1)
    sin_tab = np.concatenate([-sin, sin, -sin, sin], axis=1)
    return jnp.asarray(cos_tab, F32), jnp.asarray(sin_tab, F32)


def swap_halves(vals):
    width = vals.shape[-1]
    lane = lax.broadcasted_iota(jnp.int32, vals.shape, 1)
    up = pltpu.roll(vals, width - HD // 2, 1)
    down = pltpu.roll(vals, HD // 2, 1)
    return jnp.where(lane % HD < HD // 2, up, down)


def widen(tab, width):
    reps = width // tab.shape[1]
    return tab if reps == 1 else jnp.concatenate([tab] * reps, axis=1)


def rope(vals, cos, sin):
    width = vals.shape[-1]
    return vals * widen(cos, width) + swap_halves(vals) * widen(sin, width)


def unrope(vals, cos, sin):
    width = vals.shape[-1]
    return vals * widen(cos, width) - swap_halves(vals) * widen(sin, width)


def params(semantics=None):
    return pltpu.CompilerParams(dimension_semantics=semantics, vmem_limit_bytes=VMEM_LIMIT)


def cost(micros):
    return pl.CostEstimate(flops=0, transcendentals=0, bytes_accessed=int(micros * COST * 3.69e6))


def project_kernel(pos_ref, x_ref, gain_ref, wq_ref, wk_ref, wv_ref, cos_ref, sin_ref, og_ref, kv_ref, aux_ref):
    x = x_ref[...].astype(F32)
    inv = lax.rsqrt(jnp.mean(x * x, axis=-1, keepdims=True) + NORM_EPS)
    x1 = (x * inv * gain_ref[...]).astype(BF)
    cos, sin = cos_ref[...], sin_ref[...]
    q = rope(nn(x1, wq_ref[...]), cos, sin).astype(BF)
    q = (q.astype(F32) * (HD**-0.5)).astype(BF)
    k = rope(nn(x1, wk_ref[...]), cos, sin).astype(BF)
    v = nn(x1, wv_ref[...]).astype(BF)
    peers, _, rows, _ = aux_ref.shape
    og = og_ref[...].astype(BF)
    aux = [t[:, m * LANES : (m + 1) * LANES] for t in (q, og) for m in range(t.shape[1] // LANES)]
    db = x.shape[1] // peers
    for p in range(peers):
        kv_ref[p, 0] = k
        kv_ref[p, 1] = v
        for m in range(len(aux)):
            aux_ref[p, m] = aux[m]
        cols = x1[:, p * db : (p + 1) * db]
        if db < LANES:
            cols = jnp.concatenate([cols, jnp.zeros((rows, LANES - db), BF)], axis=1)
        aux_ref[p, len(aux)] = cols


def project(pos, peers, block_in, gain, wq, wk, wv, cos, sin, out_grad, piece):
    rows, width = block_in.shape
    planes = (wq.shape[1] + piece) // LANES + 1
    full = lambda shape: pl.BlockSpec(shape, lambda g, p: (0,) * len(shape))
    tab = pl.BlockSpec((rows, LANES), lambda g, p: (p[0], 0))
    return pl.pallas_call(
        project_kernel,
        grid_spec=pltpu.PrefetchScalarGridSpec(
            num_scalar_prefetch=1,
            grid=(1,),
            in_specs=[
                full((rows, width)),
                full((1, width)),
                full(wq.shape),
                full(wk.shape),
                full(wv.shape),
                tab,
                tab,
                pl.BlockSpec((rows, piece), lambda g, p: (0, p[1])),
            ],
            out_specs=[full((peers, 2, rows, LANES)), full((peers, planes, rows, LANES))],
        ),
        out_shape=[
            jax.ShapeDtypeStruct((peers, 2, rows, LANES), BF),
            jax.ShapeDtypeStruct((peers, planes, rows, LANES), BF),
        ],
        compiler_params=params(),
        cost_estimate=cost(3),
        name="project",
    )(pos, block_in, gain, wq, wk, wv, cos, sin, out_grad)


def attend_kernel(pos_ref, q_ref, kv_ref, out_ref):
    i = pos_ref[0]
    blocks, _, rows, kw = kv_ref.shape
    heads = kw // HD
    group = q_ref.shape[2] // HD
    n = blocks * rows
    k_all = kv_ref[:, 0].reshape(n, kw)
    v_all = kv_ref[:, 1].reshape(n, kw)
    col = lax.broadcasted_iota(jnp.int32, (group * rows, n), 1)
    row = lax.broadcasted_iota(jnp.int32, (group * rows, n), 0) % rows + i * rows
    allowed = col <= row
    for h in range(heads):
        k = k_all[:, h * HD : (h + 1) * HD]
        v = v_all[:, h * HD : (h + 1) * HD]
        q = jnp.concatenate([q_ref[h, :, g * HD : (g + 1) * HD] for g in range(group)], axis=0)
        s = jnp.where(allowed, nt(q, k), -1e30)
        top = jnp.max(s, axis=-1, keepdims=True)
        e = jnp.exp(s - top)
        total = jnp.sum(e, axis=-1, keepdims=True)
        o = (nn(e.astype(BF), v) / total).astype(BF)
        for g in range(group):
            c = (h * group + g) * HD
            out_ref[:, c : c + HD] = o[g * rows : (g + 1) * rows]


def attend(pos, aux, kv_all):
    _, _, rows, _ = aux.shape
    q_planes = kv_all.shape[3] // HD
    return pl.pallas_call(
        attend_kernel,
        grid_spec=pltpu.PrefetchScalarGridSpec(
            num_scalar_prefetch=1,
            grid=(1,),
            in_specs=[
                pl.BlockSpec((None, q_planes, rows, LANES), lambda g, p: (0, 0, 0, 0)),
                pl.BlockSpec(kv_all.shape, lambda g, p: (0, 0, 0, 0)),
            ],
            out_specs=pl.BlockSpec((rows, q_planes * LANES), lambda g, p: (0, 0)),
        ),
        out_shape=jax.ShapeDtypeStruct((rows, q_planes * LANES), BF),
        compiler_params=params(),
        cost_estimate=cost(3),
        name="attend",
    )(pos, aux, kv_all)


def mid_kernel(n_sh, *refs):
    pos_ref = refs[0]
    heads = refs[1 : n_sh + 1]
    ow = refs[n_sh + 1 : 2 * n_sh + 1]
    x_ref, gain_ref, router_ref, routes_ref, resid_ref, x2_ref, gates_ref, send_ref = refs[2 * n_sh + 1 :]
    acc = x_ref[...].astype(F32)
    for h, w in zip(heads, ow):
        acc = acc + nn(h[...], w[...])
    resid_ref[...] = acc
    inv = lax.rsqrt(jnp.mean(acc * acc, axis=-1, keepdims=True) + NORM_EPS)
    x2 = (acc * inv * gain_ref[...]).astype(BF)
    x2_ref[...] = x2
    logits = nn(x2, router_ref[...])
    lane = lax.broadcasted_iota(jnp.int32, logits.shape, 1)
    chosen = lane < 0
    for k in range(routes_ref.shape[1]):
        chosen = chosen | (routes_ref[:, k : k + 1] == lane)
    masked = jnp.where(chosen, logits, -1e30)
    e = jnp.where(chosen, jnp.exp(masked - jnp.max(masked, axis=-1, keepdims=True)), 0.0)
    gates = e / jnp.sum(e, axis=-1, keepdims=True)
    gates_ref[...] = gates
    rows, width = acc.shape
    planes = width // n_sh // LANES
    n_gate = send_ref.shape[1] - planes * rows
    g_rows = jnp.transpose(gates)[:n_gate].astype(BF)
    s = pos_ref[1]
    mine = []
    for m in range(planes):
        plane = x2[:, m * LANES : (m + 1) * LANES]
        for k in range(1, n_sh):
            at = (k * planes + m) * LANES
            plane = jnp.where(s == k, x2[:, at : at + LANES], plane)
        mine.append(plane)
    for m in range(planes):
        send_ref[0, m * rows : (m + 1) * rows] = mine[m]
    send_ref[0, planes * rows :] = g_rows


def mid(pos, n_gate, heads, ow, block_in, gain, router_pad, routes):
    rows, width = block_in.shape
    n_sh = len(heads)
    total = width // n_sh // LANES * rows + n_gate
    return pl.pallas_call(
        functools.partial(mid_kernel, n_sh),
        in_specs=[pl.BlockSpec(memory_space=pltpu.SMEM)] + [pl.BlockSpec()] * (2 * n_sh + 4),
        out_shape=[
            jax.ShapeDtypeStruct((rows, width), F32),
            jax.ShapeDtypeStruct((rows, width), BF),
            jax.ShapeDtypeStruct((rows, LANES), F32),
            jax.ShapeDtypeStruct((1, total, LANES), BF),
        ],
        compiler_params=params(),
        cost_estimate=cost(4),
        name="mid",
    )(pos, *heads, *ow, block_in, gain, router_pad, routes)


def expert_terms(pg, pu, g_out, gate):
    sig = jax.nn.sigmoid(pg)
    silu = pg * sig
    hid = silu * pu
    dh = gate * g_out
    dpg = (dh * pu * (sig * (1.0 + pg * (1.0 - sig)))).astype(BF)
    dpu = (dh * silu).astype(BF)
    return hid, dpg, dpu


def experts_own_kernel(pos_ref, x_ref, og_ref, gates_ref, wg_ref, wu_ref, wd_ref, moe_ref, ex_ref, acc_m, acc_d, acc_g):
    e = pl.program_id(0)
    n_e = pl.num_programs(0)
    width = x_ref.shape[1]

    @pl.when(e == 0)
    def _():
        acc_m[...] = jnp.zeros_like(acc_m)
        acc_d[...] = jnp.zeros_like(acc_d)
        acc_g[...] = jnp.zeros_like(acc_g)

    lane = lax.broadcasted_iota(jnp.int32, gates_ref.shape, 1)
    mine = lane == pos_ref[1] * n_e + e
    gate = jnp.sum(jnp.where(mine, gates_ref[...], 0.0), axis=-1, keepdims=True)
    x = x_ref[...]
    wg, wu, wd = wg_ref[0], wu_ref[0], wd_ref[0]
    pg, pu, g_out = nn(x, wg), nn(x, wu), nt(og_ref[...].astype(BF), wd)
    hid, dpg, dpu = expert_terms(pg, pu, g_out, gate)
    d_gate = jnp.sum(hid.astype(BF).astype(F32) * g_out, axis=-1, keepdims=True)
    acc_m[...] += nn((gate * hid).astype(BF), wd)
    acc_d[...] += nt(dpg, wg) + nt(dpu, wu)
    acc_g[...] += jnp.where(mine, d_gate, 0.0)

    @pl.when(e == n_e - 1)
    def _():
        moe_ref[...] = acc_m[...].astype(BF)
        ex_ref[:, :width] = acc_d[...].astype(BF)
        ex_ref[:, width:] = acc_g[...].astype(BF)


def experts_own(pos, x2, og, gates, wg, wu, wd):
    rows, width = x2.shape
    n_e, _, ff = wg.shape
    full = lambda shape: pl.BlockSpec(shape, lambda e, p: (0,) * len(shape))
    return pl.pallas_call(
        experts_own_kernel,
        grid_spec=pltpu.PrefetchScalarGridSpec(
            num_scalar_prefetch=1,
            grid=(n_e,),
            in_specs=[
                full((rows, width)),
                full((rows, width)),
                full((rows, LANES)),
                pl.BlockSpec((1, width, ff), lambda e, p: (e, 0, 0)),
                pl.BlockSpec((1, width, ff), lambda e, p: (e, 0, 0)),
                pl.BlockSpec((1, ff, width), lambda e, p: (e, 0, 0)),
            ],
            out_specs=[full((rows, width)), full((rows, width + LANES))],
            scratch_shapes=[
                pltpu.VMEM((rows, width), F32),
                pltpu.VMEM((rows, width), F32),
                pltpu.VMEM((rows, LANES), F32),
            ],
        ),
        out_shape=[
            jax.ShapeDtypeStruct((rows, width), BF),
            jax.ShapeDtypeStruct((rows, width + LANES), BF),
        ],
        compiler_params=params(("arbitrary",)),
        cost_estimate=cost(11),
        name="experts_own",
    )(pos, x2, og, gates, wg, wu, wd)


def back_mid_kernel(
    n_exp, ex_ref, far_ref, resid_ref, gain_ref, gates_ref, router_ref, og_ref, ow_ref, dmid_ref, send_ref, cols_ref
):
    rows, width = resid_ref.shape
    ex = ex_ref[...].astype(F32) + far_ref[...].astype(F32)
    gates = gates_ref[...]
    d_gate = ex[:, width:]
    d_logits = gates * (d_gate - jnp.sum(gates * d_gate, axis=-1, keepdims=True))
    d_norm = ex[:, :width] + nt(d_logits.astype(BF), router_ref[...])
    resid = resid_ref[...]
    inv = lax.rsqrt(jnp.mean(resid * resid, axis=-1, keepdims=True) + NORM_EPS)
    hat = resid * inv
    d_gain = jnp.sum(d_norm * hat, axis=0, keepdims=True)
    u = gain_ref[...] * d_norm
    inner = jnp.mean(u * hat, axis=-1, keepdims=True)
    d_mid = og_ref[...] + inv * (u - hat * inner)
    dmid_ref[...] = d_mid
    dmb = d_mid.astype(BF)
    d_heads = nt(dmb, ow_ref[...]).astype(BF)
    planes = d_heads.shape[1] // LANES
    gain_rows = [d_gain[:, k * LANES : (k + 1) * LANES] for k in range(width // LANES)]
    small = jnp.concatenate([jnp.transpose(d_logits)[:n_exp]] + gain_rows, axis=0).astype(BF)
    peers = send_ref.shape[0]
    db = width // peers
    for p in range(peers):
        for m in range(planes):
            send_ref[p, m * rows : (m + 1) * rows] = d_heads[:, m * LANES : (m + 1) * LANES]
        send_ref[p, planes * rows :] = small
        cols_ref[p] = dmb[:, p * db : (p + 1) * db]


def back_mid(peers, n_exp, ex, far, resid, gain, gates, router_pad, og, ow):
    rows, width = resid.shape
    total = ow.shape[0] // LANES * rows + n_exp + width // LANES
    return pl.pallas_call(
        functools.partial(back_mid_kernel, n_exp),
        out_shape=[
            jax.ShapeDtypeStruct((rows, width), F32),
            jax.ShapeDtypeStruct((peers, total, LANES), BF),
            jax.ShapeDtypeStruct((peers, rows, width // peers), BF),
        ],
        compiler_params=params(),
        cost_estimate=cost(3),
        name="back_mid",
    )(ex, far, resid, gain, gates, router_pad, og, ow)


def attend_back_kernel(
    pos_ref, q_ref, kv_ref, do_ref, cos_ref, sin_ref, wq_ref, wk_ref, wv_ref,
    dn_ref, qkvg_ref, ho_ref, qs, ks, vs, dos, dqs, hos, dkt, dvt, dqkv,
):
    i = pos_ref[0]
    blocks, _, rows, kw = kv_ref.shape
    heads = kw // HD
    group = LANES // HD
    q_planes = heads
    qw = q_planes * LANES
    n = blocks * rows
    bq = 2 * rows if n <= 1024 else rows // 2
    for j in range(blocks):
        at = slice(j * rows, (j + 1) * rows)
        kb, vb = kv_ref[j, 0], kv_ref[j, 1]
        for h in range(heads):
            ks[h, at] = kb[:, h * HD : (h + 1) * HD]
            vs[h, at] = vb[:, h * HD : (h + 1) * HD]
            for g in range(group):
                qs[h, g, at] = q_ref[j, h, :, g * HD : (g + 1) * HD]
                dos[h, g, at] = do_ref[j, h * rows : (h + 1) * rows, g * HD : (g + 1) * HD]
    dkt[...] = jnp.zeros_like(dkt)
    dvt[...] = jnp.zeros_like(dvt)

    def step(h, start, ext, full):
        k, v = ks[h, :ext], vs[h, :ext]
        q = jnp.concatenate([qs[h, g, pl.ds(start, bq)] for g in range(group)], axis=0)
        do = jnp.concatenate([dos[h, g, pl.ds(start, bq)] for g in range(group)], axis=0)
        s = nt(q, k)
        edge = s if full else s[:, ext - bq :]
        first = 0 if full else ext - bq
        col = lax.broadcasted_iota(jnp.int32, edge.shape, 1) + first
        row = lax.broadcasted_iota(jnp.int32, edge.shape, 0) % bq + start
        edge = jnp.where(col <= row, edge, -1e30)
        s = edge if first == 0 else jnp.concatenate([s[:, :first], edge], axis=1)
        top = jnp.max(s, axis=-1, keepdims=True)
        e = jnp.exp(s - top)
        p = e * (1.0 / jnp.sum(e, axis=-1, keepdims=True))
        dp = nt(do, v)
        delta = jnp.sum(p * dp, axis=-1, keepdims=True)
        ds = (p * (dp - delta)).astype(BF)
        pb = p.astype(BF)
        o = nn(pb, v)
        dq = nn(ds, k) * (HD**-0.5)
        dkt[h, :, :ext] += tn(q, ds)
        dvt[h, :, :ext] += tn(do, pb)
        for g in range(group):
            dqs[h, g, pl.ds(start, bq)] = dq[g * bq : (g + 1) * bq]
            hos[h, g, pl.ds(start, bq)] = o[g * bq : (g + 1) * bq].astype(BF)

    def per_head(h, carry):
        if n <= 1024:
            for r in range(n // bq):
                step(h, r * bq, (r + 1) * bq, False)
        else:

            def loop(r, c):
                step(h, pl.multiple_of(r * bq, bq), n, True)
                return c

            lax.fori_loop(0, n // bq, loop, 0)
        return carry

    lax.fori_loop(0, heads, per_head, 0)
    pieces = [(h, g) for h in range(heads) for g in range(group)]
    qkvg_ref[...] = jnp.zeros_like(qkvg_ref)

    def per_block(j, carry):
        at = pl.ds(pl.multiple_of(j * rows, rows), rows)
        cos, sin = cos_ref[at], sin_ref[at]
        ho_ref[j] = jnp.concatenate([hos[h, g, at] for h, g in pieces], axis=1)
        dq = jnp.concatenate([dqs[h, g, at] for h, g in pieces], axis=1)
        dk = jnp.transpose(jnp.concatenate([dkt[h, :, at] for h in range(heads)], axis=0))
        dv = jnp.transpose(jnp.concatenate([dvt[h, :, at] for h in range(heads)], axis=0))
        out = jnp.concatenate([unrope(dq, cos, sin), unrope(dk, cos, sin), dv], axis=1).astype(BF)
        dqkv[j] = out
        qkvg_ref[...] += tn(q_ref[j, q_ref.shape[1] - 1], out)
        return carry

    lax.fori_loop(0, blocks, per_block, 0)
    own = dqkv[i]
    width = wq_ref.shape[0]
    db = width // blocks
    dn_ref[:, :width] = (
        nt(own[:, :qw], wq_ref[...]) + nt(own[:, qw : qw + kw], wk_ref[...]) + nt(own[:, qw + kw :], wv_ref[...])
    ).astype(BF)
    mine = pl.ds(pl.multiple_of(i * db, db), db)
    w_rows = jnp.concatenate([wq_ref[mine], wk_ref[mine], wv_ref[mine]], axis=1).astype(F32)
    gain = jnp.sum(qkvg_ref[:db] * w_rows, axis=1, keepdims=True)
    if db < rows:
        gain = jnp.concatenate([gain, jnp.zeros((rows - db, 1), F32)], axis=0)
    dn_ref[:, width:] = jnp.broadcast_to(gain, (rows, LANES)).astype(BF)


def attend_back(pos, q_all, kv_all, do_all, cos, sin, wq, wk, wv):
    blocks, _, rows, kw = kv_all.shape
    width, qw = wq.shape
    heads, group = kw // HD, LANES // HD
    n = blocks * rows
    return pl.pallas_call(
        attend_back_kernel,
        in_specs=[pl.BlockSpec(memory_space=pltpu.SMEM)] + [pl.BlockSpec()] * 8,
        out_shape=[
            jax.ShapeDtypeStruct((rows, width + LANES), BF),
            jax.ShapeDtypeStruct((LANES, qw + 2 * kw), F32),
            jax.ShapeDtypeStruct((blocks, rows, qw), BF),
        ],
        scratch_shapes=[
            pltpu.VMEM((heads, group, n, HD), BF),
            pltpu.VMEM((heads, n, HD), BF),
            pltpu.VMEM((heads, n, HD), BF),
            pltpu.VMEM((heads, group, n, HD), BF),
            pltpu.VMEM((heads, group, n, HD), F32),
            pltpu.VMEM((heads, group, n, HD), BF),
            pltpu.VMEM((heads, HD, n), F32),
            pltpu.VMEM((heads, HD, n), F32),
            pltpu.VMEM((blocks, rows, qw + 2 * kw), BF),
        ],
        compiler_params=params(),
        cost_estimate=cost(18),
        name="attend_back",
    )(pos, q_all, kv_all, do_all, cos, sin, wq, wk, wv)


def experts_all_kernel(n_sh, rows, *refs):
    pos_ref, refs = refs[0], refs[1:]
    xs, ogs = refs[:n_sh], refs[n_sh : 2 * n_sh]
    gates_ref = refs[2 * n_sh]
    base = 2 * n_sh + 1
    wgs, wus, wds = (refs[base + k * n_sh : base + (k + 1) * n_sh] for k in range(3))
    gg_ref, ug_ref, dg_ref, xc_ref, acc = refs[base + 3 * n_sh :]
    e, c = pl.program_id(0), pl.program_id(1)
    nb = xs[0].shape[0]
    tb = nb * rows
    planes = wgs[0].shape[1] // LANES
    lane = lax.broadcasted_iota(jnp.int32, (tb, LANES), 1)
    mine = lane == pos_ref[1] * pl.num_programs(0) + e
    gate = jnp.sum(jnp.where(mine, gates_ref[...], 0.0), axis=-1, keepdims=True)
    x_planes = [[x[:, m * rows : (m + 1) * rows].reshape(tb, LANES) for m in range(planes)] for x in xs]
    block = [pos_ref[3 + c * nb + t] for t in range(nb)]
    o_planes = [[jnp.concatenate([o[j, m] for j in block], axis=0) for m in range(planes)] for o in ogs]
    xv = [jnp.concatenate(p, axis=1) for p in x_planes]
    ov = [jnp.concatenate(p, axis=1) for p in o_planes]
    pg = sum(nn(x, w[0]) for x, w in zip(xv, wgs))
    pu = sum(nn(x, w[0]) for x, w in zip(xv, wus))
    g_out = sum(nt(o, w[0]) for o, w in zip(ov, wds))
    hid, dpg, dpu = expert_terms(pg, pu, g_out, gate)
    hg = (gate * hid).astype(BF)
    plane = pos_ref[2]
    xc, oc = x_planes[0][0], o_planes[0][0]
    for b in range(n_sh):
        for m in range(planes):
            hit = plane == (pos_ref[1] ^ b) * planes + m
            xc = jnp.where(hit, x_planes[b][m], xc)
            oc = jnp.where(hit, o_planes[b][m], oc)
    for t, j in enumerate(block):
        xc_ref[j] = xc[t * rows : (t + 1) * rows]
    gg, ug, dg = tn(xc, dpg), tn(xc, dpu), tn(oc, hg)

    @pl.when(c == 0)
    def _():
        gg_ref[0] = gg
        ug_ref[0] = ug
        acc[...] = dg

    @pl.when(c > 0)
    def _():
        gg_ref[0] += gg
        ug_ref[0] += ug
        acc[...] += dg

    @pl.when(c == pl.num_programs(1) - 1)
    def _():
        dg_ref[0] = jnp.transpose(acc[...])


def experts_all(pos, xs, ogs, gates, wg, wu, wd):
    n_sh = len(xs)
    blocks, total, _ = xs[0].shape
    _, planes, rows, _ = ogs[0].shape
    piece = planes * LANES
    n = blocks * rows
    n_e, width, ff = wg.shape
    nb = math.gcd(blocks, 4)
    x_tok = pl.BlockSpec((nb, total, LANES), lambda e, c, p: (c, 0, 0))
    o_tok = pl.BlockSpec(ogs[0].shape, lambda e, c, p: (0, 0, 0, 0))
    row_w = lambda b: pl.BlockSpec((1, piece, ff), lambda e, c, p, b=b: (e, p[1] ^ b, 0))
    col_w = lambda b: pl.BlockSpec((1, ff, piece), lambda e, c, p, b=b: (e, 0, p[1] ^ b))
    out = pl.BlockSpec((1, LANES, ff), lambda e, c, p: (e, 0, 0))
    out_t = pl.BlockSpec((1, ff, LANES), lambda e, c, p: (e, 0, 0))
    sh = range(n_sh)
    return pl.pallas_call(
        functools.partial(experts_all_kernel, n_sh, rows),
        grid_spec=pltpu.PrefetchScalarGridSpec(
            num_scalar_prefetch=1,
            grid=(n_e, blocks // nb),
            in_specs=[x_tok for _ in sh]
            + [o_tok for _ in sh]
            + [pl.BlockSpec((nb * rows, LANES), lambda e, c, p: (c, 0))]
            + [row_w(b) for b in sh]
            + [row_w(b) for b in sh]
            + [col_w(b) for b in sh],
            out_specs=[out, out, out_t, pl.BlockSpec((blocks, rows, LANES), lambda e, c, p: (0, 0, 0))],
            scratch_shapes=[pltpu.VMEM((LANES, ff), F32)],
        ),
        out_shape=[jax.ShapeDtypeStruct((n_e, LANES, ff), F32)] * 2
        + [jax.ShapeDtypeStruct((n_e, ff, LANES), F32), jax.ShapeDtypeStruct((blocks, rows, LANES), BF)],
        compiler_params=params(("arbitrary", "arbitrary")),
        cost_estimate=cost(25),
        name="experts_all",
    )(pos, *xs, *ogs, gates, *[wg] * n_sh, *[wu] * n_sh, *[wd] * n_sh)


def finish_kernel(dn_ref, far_ref, x_ref, gain_ref, dmid_ref, out_ref, dgain_ref):
    width = x_ref.shape[1]
    dn = dn_ref[...].astype(F32) + far_ref[...].astype(F32)
    dgain_ref[...] = dn[:, width:]
    x = x_ref[...].astype(F32)
    inv = lax.rsqrt(jnp.mean(x * x, axis=-1, keepdims=True) + NORM_EPS)
    hat = x * inv
    u = gain_ref[...] * dn[:, :width]
    out_ref[...] = dmid_ref[...] + inv * (u - hat * jnp.mean(u * hat, axis=-1, keepdims=True))


def finish(dn, far, block_in, gain, d_mid):
    rows, width = block_in.shape
    return pl.pallas_call(
        finish_kernel,
        out_shape=[jax.ShapeDtypeStruct((rows, width), F32), jax.ShapeDtypeStruct((rows, LANES), F32)],
        compiler_params=params(),
        cost_estimate=cost(2),
        name="finish",
    )(dn, far, block_in, gain, d_mid)


def exchange(x, bit):
    size = lax.axis_size("shard")
    return lax.ppermute(x, "shard", [(j, j ^ bit) for j in range(size)])


def gather_ctx(x):
    size = lax.axis_size("ctx")
    bit = size // 2
    while bit:
        far = lax.ppermute(x, "ctx", [(j, j ^ bit) for j in range(size)])
        x = jnp.concatenate([x, far], axis=0)
        bit //= 2
    return x


def ctx_order(size):
    order = [0]
    bit = size // 2
    while bit:
        order = order + [o ^ bit for o in order]
        bit //= 2
    return jnp.array(order, jnp.int32) ^ lax.axis_index("ctx")


def swap_ctx(x):
    return lax.all_to_all(x, "ctx", 0, 0, tiled=True)


def gather_shard(x):
    found = {0: x}
    bit = lax.axis_size("shard") // 2
    while bit:
        for off in list(found):
            found[off ^ bit] = exchange(found[off], bit)
        bit //= 2
    return [found[b] for b in range(len(found))]


def halves_shard(x):
    last = lax.axis_size("shard") // 2
    bit = 1
    while bit < last:
        x = (x.astype(F32) + exchange(x, bit).astype(F32)).astype(x.dtype)
        bit *= 2
    return x, exchange(x, last)


def after(x, token):
    return lax.optimization_barrier((x, token))[0]


def body(
    block_in,
    attn_gain,
    q_weight,
    k_weight,
    v_weight,
    o_weight,
    moe_gain,
    router_weight,
    expert_gate,
    expert_up,
    expert_down,
    routes,
    out_grad,
):
    rows, width = block_in.shape
    n_ctx, n_sh = lax.axis_size("ctx"), lax.axis_size("shard")
    seq_len = rows * n_ctx
    n_exp = router_weight.shape[1]
    db = width // n_ctx
    qw, kw = q_weight.shape[1], k_weight.shape[1]
    q_planes = qw // LANES
    i, s = lax.axis_index("ctx"), lax.axis_index("shard")
    lane_at = (i * db) % LANES
    pos = jnp.concatenate([jnp.stack([i, s, (i * db) // LANES]).astype(jnp.int32), ctx_order(n_ctx)])
    cos, sin = rope_constants(seq_len)
    gain_one = attn_gain.reshape(1, width)
    gain_two = moe_gain.reshape(1, width)
    router_pad = jnp.pad(router_weight, ((0, 0), (0, LANES - n_exp)))

    piece = width // n_sh
    kv_send, aux_send = project(
        pos, n_ctx, block_in, gain_one, q_weight, k_weight, v_weight, cos, sin, out_grad, piece
    )
    kv_all = swap_ctx(kv_send)
    ow = gather_shard(o_weight)
    aux_all = swap_ctx(after(aux_send, kv_all))
    heads = attend(pos, aux_send, kv_all)
    resid_mid, x2, gates, x2_send = mid(
        pos, n_exp, gather_shard(heads), ow, block_in, gain_two, router_pad, routes
    )
    x2_all = gather_ctx(x2_send)
    moe_part, ex_part = experts_own(pos, x2, out_grad, gates, expert_gate, expert_up, expert_down)
    d_mid, back_send, dmid_send = back_mid(
        n_ctx, n_exp, *halves_shard(ex_part), resid_mid, gain_two, gates, router_pad, out_grad, o_weight
    )
    back_all = swap_ctx(after(back_send, aux_all))
    moe_near, moe_far = halves_shard(moe_part)
    block_out = resid_mid + moe_near.astype(F32) + moe_far.astype(F32)
    dn_part, qkv_grad, heads_all = attend_back(
        pos, aux_all, kv_all, back_all, cos, sin, q_weight, k_weight, v_weight
    )
    in_grad, gain_sum = finish(*halves_shard(dn_part), block_in, gain_one, d_mid)
    attn_gain_grad = gain_sum[:db, 0] / lax.dynamic_slice_in_dim(attn_gain, i * db, db, 0)
    q_grad, k_grad, v_grad = qkv_grad[:db, :qw], qkv_grad[:db, qw : qw + kw], qkv_grad[:db, qw + kw :]

    dmid_cols = swap_ctx(after(dmid_send, back_all))
    o_grad = tn(heads_all.reshape(seq_len, qw), dmid_cols.reshape(seq_len, db))

    gates_all = x2_all[:, piece // LANES * rows :].swapaxes(1, 2).reshape(seq_len, n_exp).astype(F32)
    gates_all = jnp.pad(gates_all, ((0, 0), (0, LANES - n_exp)))
    ogs = gather_shard(aux_all[:, qw // LANES : -1])
    xs = gather_shard(x2_all[:, : piece // LANES * rows])
    gate_grad, up_grad, down_grad, x_cols = experts_all(
        pos, xs, ogs, gates_all, expert_gate, expert_up, expert_down
    )
    small = back_all[:, q_planes * rows :]
    d_logits_all = small[:, :n_exp].swapaxes(1, 2).reshape(seq_len, n_exp)
    router_grad = tn(x_cols.reshape(seq_len, LANES), d_logits_all)
    if db < LANES:
        gate_grad = lax.dynamic_slice_in_dim(gate_grad, lane_at, db, 1)
        up_grad = lax.dynamic_slice_in_dim(up_grad, lane_at, db, 1)
        down_grad = lax.dynamic_slice_in_dim(down_grad, lane_at, db, 2)
        router_grad = lax.dynamic_slice_in_dim(router_grad, lane_at, db, 0)
    moe_gain_sum = jnp.sum(small[:, n_exp:].astype(F32), axis=0).reshape(width)
    moe_gain_grad = lax.dynamic_slice_in_dim(moe_gain_sum, i * db, db, 0)
    return (
        block_out,
        in_grad,
        attn_gain_grad,
        q_grad,
        k_grad,
        v_grad,
        o_grad,
        moe_gain_grad,
        router_grad,
        gate_grad,
        up_grad,
        down_grad,
    )


def solution(mesh):
    in_specs = (
        P("ctx", None),
        P(),
        P(None, "shard"),
        P(None, "shard"),
        P(None, "shard"),
        P("shard", None),
        P(),
        P(),
        P("shard", None, None),
        P("shard", None, None),
        P("shard", None, None),
        P("ctx", None),
        P("ctx", None),
    )
    out_specs = (
        P("ctx", None),
        P("ctx", None),
        P("ctx"),
        P("ctx", "shard"),
        P("ctx", "shard"),
        P("ctx", "shard"),
        P("shard", "ctx"),
        P("ctx"),
        P("ctx", None),
        P("shard", "ctx", None),
        P("shard", "ctx", None),
        P("shard", None, "ctx"),
    )
    return jax.shard_map(body, mesh=mesh, in_specs=in_specs, out_specs=out_specs, check_vma=False)
```

```python
import functools
import math

import jax
import jax.numpy as jnp
import numpy as np
from jax import lax
from jax.experimental import pallas as pl
from jax.experimental.pallas import tpu as pltpu
from jax.sharding import PartitionSpec as P

HD = 64
NORM_EPS = 1e-06
ROPE_BASE = 10000.0
BF = jnp.bfloat16
F32 = jnp.float32
LANES = 128
COST = 0.05
VMEM_LIMIT = 56 * 1024 * 1024


def nn(a, b):
    return lax.dot_general(a, b, (((1,), (0,)), ((), ())), preferred_element_type=F32)


def nt(a, b):
    return lax.dot_general(a, b, (((1,), (1,)), ((), ())), preferred_element_type=F32)


def tn(a, b):
    return lax.dot_general(a, b, (((0,), (0,)), ((), ())), preferred_element_type=F32)


def rope_constants(seq_len):
    half = HD // 2
    steps = np.arange(half, dtype=np.float32) * np.float32(2.0 / HD)
    inv_freq = np.exp(np.float32(-math.log(ROPE_BASE)) * steps).astype(np.float32)
    angles = np.arange(seq_len, dtype=np.float32)[:, None] * inv_freq[None, :]
    cos, sin = np.cos(angles), np.sin(angles)
    cos_tab = np.concatenate([cos, cos, cos, cos], axis=1)
    sin_tab = np.concatenate([-sin, sin, -sin, sin], axis=1)
    return jnp.asarray(cos_tab, F32), jnp.asarray(sin_tab, F32)


def swap_halves(vals):
    width = vals.shape[-1]
    lane = lax.broadcasted_iota(jnp.int32, vals.shape, 1)
    up = pltpu.roll(vals, width - HD // 2, 1)
    down = pltpu.roll(vals, HD // 2, 1)
    return jnp.where(lane % HD < HD // 2, up, down)


def widen(tab, width):
    reps = width // tab.shape[1]
    return tab if reps == 1 else jnp.concatenate([tab] * reps, axis=1)


def rope(vals, cos, sin):
    width = vals.shape[-1]
    return vals * widen(cos, width) + swap_halves(vals) * widen(sin, width)


def unrope(vals, cos, sin):
    width = vals.shape[-1]
    return vals * widen(cos, width) - swap_halves(vals) * widen(sin, width)


def params(semantics=None):
    return pltpu.CompilerParams(dimension_semantics=semantics, vmem_limit_bytes=VMEM_LIMIT)


def cost(micros):
    return pl.CostEstimate(flops=0, transcendentals=0, bytes_accessed=int(micros * COST * 3.69e6))


def project_kernel(pos_ref, x_ref, gain_ref, wq_ref, wk_ref, wv_ref, cos_ref, sin_ref, kv_ref, aux_ref):
    x = x_ref[...].astype(F32)
    inv = lax.rsqrt(jnp.mean(x * x, axis=-1, keepdims=True) + NORM_EPS)
    x1 = (x * inv * gain_ref[...]).astype(BF)
    cos, sin = cos_ref[...], sin_ref[...]
    q = rope(nn(x1, wq_ref[...]), cos, sin).astype(BF)
    q = (q.astype(F32) * (HD**-0.5)).astype(BF)
    k = rope(nn(x1, wk_ref[...]), cos, sin).astype(BF)
    v = nn(x1, wv_ref[...]).astype(BF)
    peers, _, rows, _ = aux_ref.shape
    aux = [q[:, m * LANES : (m + 1) * LANES] for m in range(q.shape[1] // LANES)]
    db = x.shape[1] // peers
    for p in range(peers):
        kv_ref[p, 0] = k
        kv_ref[p, 1] = v
        for m in range(len(aux)):
            aux_ref[p, m] = aux[m]
        cols = x1[:, p * db : (p + 1) * db]
        if db < LANES:
            cols = jnp.concatenate([cols, jnp.zeros((rows, LANES - db), BF)], axis=1)
        aux_ref[p, len(aux)] = cols


def project(pos, peers, block_in, gain, wq, wk, wv, cos, sin):
    rows, width = block_in.shape
    planes = wq.shape[1] // LANES + 1
    full = lambda shape: pl.BlockSpec(shape, lambda g, p: (0,) * len(shape))
    tab = pl.BlockSpec((rows, LANES), lambda g, p: (p[0], 0))
    return pl.pallas_call(
        project_kernel,
        grid_spec=pltpu.PrefetchScalarGridSpec(
            num_scalar_prefetch=1,
            grid=(1,),
            in_specs=[
                full((rows, width)),
                full((1, width)),
                full(wq.shape),
                full(wk.shape),
                full(wv.shape),
                tab,
                tab,
            ],
            out_specs=[full((peers, 2, rows, LANES)), full((peers, planes, rows, LANES))],
        ),
        out_shape=[
            jax.ShapeDtypeStruct((peers, 2, rows, LANES), BF),
            jax.ShapeDtypeStruct((peers, planes, rows, LANES), BF),
        ],
        compiler_params=params(),
        cost_estimate=cost(3),
        name="project",
    )(pos, block_in, gain, wq, wk, wv, cos, sin)


def attend_kernel(pos_ref, q_ref, kv_ref, out_ref):
    i = pos_ref[0]
    blocks, _, rows, kw = kv_ref.shape
    heads = kw // HD
    group = q_ref.shape[2] // HD
    n = blocks * rows
    k_all = kv_ref[:, 0].reshape(n, kw)
    v_all = kv_ref[:, 1].reshape(n, kw)
    col = lax.broadcasted_iota(jnp.int32, (group * rows, n), 1)
    row = lax.broadcasted_iota(jnp.int32, (group * rows, n), 0) % rows + i * rows
    allowed = col <= row
    for h in range(heads):
        k = k_all[:, h * HD : (h + 1) * HD]
        v = v_all[:, h * HD : (h + 1) * HD]
        q = jnp.concatenate([q_ref[h, :, g * HD : (g + 1) * HD] for g in range(group)], axis=0)
        s = jnp.where(allowed, nt(q, k), -1e30)
        top = jnp.max(s, axis=-1, keepdims=True)
        e = jnp.exp(s - top)
        total = jnp.sum(e, axis=-1, keepdims=True)
        o = (nn(e.astype(BF), v) / total).astype(BF)
        for g in range(group):
            c = (h * group + g) * HD
            out_ref[:, c : c + HD] = o[g * rows : (g + 1) * rows]


def attend(pos, aux, kv_all):
    _, _, rows, _ = aux.shape
    q_planes = kv_all.shape[3] // HD
    return pl.pallas_call(
        attend_kernel,
        grid_spec=pltpu.PrefetchScalarGridSpec(
            num_scalar_prefetch=1,
            grid=(1,),
            in_specs=[
                pl.BlockSpec((None, q_planes, rows, LANES), lambda g, p: (0, 0, 0, 0)),
                pl.BlockSpec(kv_all.shape, lambda g, p: (0, 0, 0, 0)),
            ],
            out_specs=pl.BlockSpec((rows, q_planes * LANES), lambda g, p: (0, 0)),
        ),
        out_shape=jax.ShapeDtypeStruct((rows, q_planes * LANES), BF),
        compiler_params=params(),
        cost_estimate=cost(3),
        name="attend",
    )(pos, aux, kv_all)


def mid_kernel(n_sh, *refs):
    pos_ref = refs[0]
    heads = refs[1 : n_sh + 1]
    ow = refs[n_sh + 1 : 2 * n_sh + 1]
    x_ref, gain_ref, router_ref, routes_ref, resid_ref, x2_ref, gates_ref, send_ref = refs[2 * n_sh + 1 :]
    acc = x_ref[...].astype(F32)
    for h, w in zip(heads, ow):
        acc = acc + nn(h[...], w[...])
    resid_ref[...] = acc
    inv = lax.rsqrt(jnp.mean(acc * acc, axis=-1, keepdims=True) + NORM_EPS)
    x2 = (acc * inv * gain_ref[...]).astype(BF)
    x2_ref[...] = x2
    logits = nn(x2, router_ref[...])
    lane = lax.broadcasted_iota(jnp.int32, logits.shape, 1)
    chosen = lane < 0
    for k in range(routes_ref.shape[1]):
        chosen = chosen | (routes_ref[:, k : k + 1] == lane)
    masked = jnp.where(chosen, logits, -1e30)
    e = jnp.where(chosen, jnp.exp(masked - jnp.max(masked, axis=-1, keepdims=True)), 0.0)
    gates = e / jnp.sum(e, axis=-1, keepdims=True)
    gates_ref[...] = gates
    rows, width = acc.shape
    planes = width // n_sh // LANES
    n_gate = send_ref.shape[1] - planes * rows
    g_rows = jnp.transpose(gates)[:n_gate].astype(BF)
    s = pos_ref[1]
    mine = []
    for m in range(planes):
        plane = x2[:, m * LANES : (m + 1) * LANES]
        for k in range(1, n_sh):
            at = (k * planes + m) * LANES
            plane = jnp.where(s == k, x2[:, at : at + LANES], plane)
        mine.append(plane)
    for m in range(planes):
        send_ref[0, m * rows : (m + 1) * rows] = mine[m]
    send_ref[0, planes * rows :] = g_rows


def mid(pos, n_gate, heads, ow, block_in, gain, router_pad, routes):
    rows, width = block_in.shape
    n_sh = len(heads)
    total = width // n_sh // LANES * rows + n_gate
    return pl.pallas_call(
        functools.partial(mid_kernel, n_sh),
        in_specs=[pl.BlockSpec(memory_space=pltpu.SMEM)] + [pl.BlockSpec()] * (2 * n_sh + 4),
        out_shape=[
            jax.ShapeDtypeStruct((rows, width), F32),
            jax.ShapeDtypeStruct((rows, width), BF),
            jax.ShapeDtypeStruct((rows, LANES), F32),
            jax.ShapeDtypeStruct((1, total, LANES), BF),
        ],
        compiler_params=params(),
        cost_estimate=cost(4),
        name="mid",
    )(pos, *heads, *ow, block_in, gain, router_pad, routes)


def expert_terms(pg, pu, g_out, gate):
    sig = 0.5 + 0.5 * jnp.tanh(0.5 * pg)
    silu = pg * sig
    hid = silu * pu
    dh = gate * g_out
    dpg = (dh * pu * (sig * (1.0 + pg * (1.0 - sig)))).astype(BF)
    dpu = (dh * silu).astype(BF)
    return hid, dpg, dpu


def experts_own_kernel(pos_ref, x_ref, og_ref, gates_ref, wg_ref, wu_ref, wd_ref, moe_ref, ex_ref, acc_m, acc_d, acc_g):
    e = pl.program_id(0)
    n_e = pl.num_programs(0)
    width = x_ref.shape[1]

    @pl.when(e == 0)
    def _():
        acc_m[...] = jnp.zeros_like(acc_m)
        acc_d[...] = jnp.zeros_like(acc_d)
        acc_g[...] = jnp.zeros_like(acc_g)

    lane = lax.broadcasted_iota(jnp.int32, gates_ref.shape, 1)
    mine = lane == pos_ref[1] * n_e + e
    gate = jnp.sum(jnp.where(mine, gates_ref[...], 0.0), axis=-1, keepdims=True)
    x = x_ref[...]
    wg, wu, wd = wg_ref[0], wu_ref[0], wd_ref[0]
    pg, pu, g_out = nn(x, wg), nn(x, wu), nt(og_ref[...].astype(BF), wd)
    hid, dpg, dpu = expert_terms(pg, pu, g_out, gate)
    d_gate = jnp.sum(hid.astype(BF).astype(F32) * g_out, axis=-1, keepdims=True)
    acc_m[...] += nn((gate * hid).astype(BF), wd)
    acc_d[...] += nt(dpg, wg) + nt(dpu, wu)
    acc_g[...] += jnp.where(mine, d_gate, 0.0)

    @pl.when(e == n_e - 1)
    def _():
        moe_ref[...] = acc_m[...].astype(BF)
        ex_ref[:, :width] = acc_d[...].astype(BF)
        ex_ref[:, width:] = acc_g[...].astype(BF)


def experts_own(pos, x2, og, gates, wg, wu, wd):
    rows, width = x2.shape
    n_e, _, ff = wg.shape
    full = lambda shape: pl.BlockSpec(shape, lambda e, p: (0,) * len(shape))
    return pl.pallas_call(
        experts_own_kernel,
        grid_spec=pltpu.PrefetchScalarGridSpec(
            num_scalar_prefetch=1,
            grid=(n_e,),
            in_specs=[
                full((rows, width)),
                full((rows, width)),
                full((rows, LANES)),
                pl.BlockSpec((1, width, ff), lambda e, p: (e, 0, 0)),
                pl.BlockSpec((1, width, ff), lambda e, p: (e, 0, 0)),
                pl.BlockSpec((1, ff, width), lambda e, p: (e, 0, 0)),
            ],
            out_specs=[full((rows, width)), full((rows, width + LANES))],
            scratch_shapes=[
                pltpu.VMEM((rows, width), F32),
                pltpu.VMEM((rows, width), F32),
                pltpu.VMEM((rows, LANES), F32),
            ],
        ),
        out_shape=[
            jax.ShapeDtypeStruct((rows, width), BF),
            jax.ShapeDtypeStruct((rows, width + LANES), BF),
        ],
        compiler_params=params(("arbitrary",)),
        cost_estimate=cost(11),
        name="experts_own",
    )(pos, x2, og, gates, wg, wu, wd)


def back_mid_kernel(
    n_exp, ex_ref, far_ref, resid_ref, gain_ref, gates_ref, router_ref, og_ref, ow_ref, dmid_ref, send_ref
):
    rows, width = resid_ref.shape
    ex = ex_ref[...].astype(F32) + far_ref[...].astype(F32)
    gates = gates_ref[...]
    d_gate = ex[:, width:]
    d_logits = gates * (d_gate - jnp.sum(gates * d_gate, axis=-1, keepdims=True))
    d_norm = ex[:, :width] + nt(d_logits.astype(BF), router_ref[...])
    resid = resid_ref[...]
    inv = lax.rsqrt(jnp.mean(resid * resid, axis=-1, keepdims=True) + NORM_EPS)
    hat = resid * inv
    d_gain = jnp.sum(d_norm * hat, axis=0, keepdims=True)
    u = gain_ref[...] * d_norm
    inner = jnp.mean(u * hat, axis=-1, keepdims=True)
    d_mid = og_ref[...] + inv * (u - hat * inner)
    dmid_ref[...] = d_mid
    dmb = d_mid.astype(BF)
    d_heads = nt(dmb, ow_ref[...]).astype(BF)
    planes = d_heads.shape[1] // LANES
    gain_rows = [d_gain[:, k * LANES : (k + 1) * LANES] for k in range(width // LANES)]
    small = jnp.concatenate([jnp.transpose(d_logits)[:n_exp]] + gain_rows, axis=0).astype(BF)
    peers = send_ref.shape[0]
    db = width // peers
    for p in range(peers):
        for m in range(planes):
            send_ref[p, m * rows : (m + 1) * rows] = d_heads[:, m * LANES : (m + 1) * LANES]
        cols = dmb[:, p * db : (p + 1) * db]
        if db < LANES:
            cols = jnp.concatenate([cols, jnp.zeros((rows, LANES - db), BF)], axis=1)
        send_ref[p, planes * rows : (planes + 1) * rows] = cols
        send_ref[p, (planes + 1) * rows :] = small


def back_mid(peers, n_exp, ex, far, resid, gain, gates, router_pad, og, ow):
    rows, width = resid.shape
    total = (ow.shape[0] // LANES + 1) * rows + n_exp + width // LANES
    return pl.pallas_call(
        functools.partial(back_mid_kernel, n_exp),
        out_shape=[
            jax.ShapeDtypeStruct((rows, width), F32),
            jax.ShapeDtypeStruct((peers, total, LANES), BF),
        ],
        compiler_params=params(),
        cost_estimate=cost(3),
        name="back_mid",
    )(ex, far, resid, gain, gates, router_pad, og, ow)


def block_probs(q, k, start, first, bq):
    s = nt(q, k)
    edge = s[:, first:]
    col = lax.broadcasted_iota(jnp.int32, edge.shape, 1) + first
    row = lax.broadcasted_iota(jnp.int32, edge.shape, 0) % bq + start
    edge = jnp.where(col <= row, edge, -1e30)
    s = edge if first == 0 else jnp.concatenate([s[:, :first], edge], axis=1)
    e = jnp.exp(s - jnp.max(s, axis=-1, keepdims=True))
    return e, 1.0 / jnp.sum(e, axis=-1, keepdims=True)


def load_heads(dst, block, j, h):
    rows = block.shape[0]
    for g in range(LANES // HD):
        dst[h, g, j * rows : (j + 1) * rows] = block[:, g * HD : (g + 1) * HD]


def load_keys(ks, vs, kv_ref):
    blocks, _, rows, kw = kv_ref.shape
    for j in range(blocks):
        for h in range(kw // HD):
            ks[h, j * rows : (j + 1) * rows] = kv_ref[j, 0, :, h * HD : (h + 1) * HD]
            vs[h, j * rows : (j + 1) * rows] = kv_ref[j, 1, :, h * HD : (h + 1) * HD]


def stacked(src, h, start, bq):
    return jnp.concatenate([src[h, g, pl.ds(start, bq)] for g in range(LANES // HD)], axis=0)


def attend_back_kernel(n_exp, *refs):
    pos_ref, q_ref, kv_ref, do_ref, cos_ref, sin_ref, wq_ref, wk_ref, wv_ref, gcol_ref, moe_ref = refs[:11]
    dn_ref, qkvg_ref, og_ref, mg_ref, qs, ks, vs, dos, dqs, dkt, dvt, dqkv, hos, hfull = refs[11:]
    i = pos_ref[0]
    blocks, _, rows, kw = kv_ref.shape
    heads = kw // HD
    group = LANES // HD
    qw = heads * LANES
    n = blocks * rows
    bq = 4 * rows if n <= 1024 else rows // 2
    load_keys(ks, vs, kv_ref)
    for j in range(blocks):
        for h in range(heads):
            load_heads(qs, q_ref[j, h], j, h)
            load_heads(dos, do_ref[j, h * rows : (h + 1) * rows], j, h)
    dkt[...] = jnp.zeros_like(dkt)
    dvt[...] = jnp.zeros_like(dvt)

    def step(h, start, ext, first):
        k, v = ks[h, :ext], vs[h, :ext]
        q, do = stacked(qs, h, start, bq), stacked(dos, h, start, bq)
        e, inv = block_probs(q, k, start, first, bq)
        p = e * inv
        pb = p.astype(BF)
        o = nn(pb, v).astype(BF)
        delta = jnp.sum(do.astype(F32) * o.astype(F32), axis=-1, keepdims=True)
        ds = (p * (nt(do, v) - delta)).astype(BF)
        dq = nn(ds, k) * (HD**-0.5)
        dkt[h, :, :ext] += tn(q, ds)
        dvt[h, :, :ext] += tn(do, pb)
        for g in range(group):
            dqs[h, g, pl.ds(start, bq)] = dq[g * bq : (g + 1) * bq]
            hos[h, g, pl.ds(start, bq)] = o[g * bq : (g + 1) * bq]

    def per_head(h, carry):
        if n <= 1024:
            for r in range(n // bq):
                step(h, r * bq, (r + 1) * bq, r * bq)
        else:

            def loop(r, c):
                step(h, pl.multiple_of(r * bq, bq), n, 0)
                return c

            lax.fori_loop(0, n // bq, loop, 0)
        return carry

    lax.fori_loop(0, heads, per_head, 0)
    pieces = [(h, g) for h in range(heads) for g in range(group)]
    small = (heads + 1) * rows
    mg_ref[...] = jnp.sum(do_ref[:, small + n_exp :].astype(F32), axis=0)

    def per_block(j, carry):
        at = pl.ds(pl.multiple_of(j * rows, rows), rows)
        cos, sin = cos_ref[at], sin_ref[at]
        hfull[at] = jnp.concatenate([hos[h, g, at] for h, g in pieces], axis=1)
        dq = jnp.concatenate([dqs[h, g, at] for h, g in pieces], axis=1)
        dk = jnp.transpose(jnp.concatenate([dkt[h, :, at] for h in range(heads)], axis=0))
        dv = jnp.transpose(jnp.concatenate([dvt[h, :, at] for h in range(heads)], axis=0))
        out = jnp.concatenate([unrope(dq, cos, sin), unrope(dk, cos, sin), dv], axis=1).astype(BF)
        dqkv[j] = out
        return carry

    lax.fori_loop(0, blocks, per_block, 0, unroll=2)
    qkvg_ref[...] = tn(q_ref[:, q_ref.shape[1] - 1].reshape(n, LANES), dqkv[...].reshape(n, qw + 2 * kw))
    og_ref[...] = tn(hfull[...], do_ref[:, heads * rows : (heads + 1) * rows].reshape(n, LANES))
    own = dqkv[i]
    width = wq_ref.shape[0]
    db = width // blocks
    dn_ref[:, :width] = (
        nt(own[:, :qw], wq_ref[...]) + nt(own[:, qw : qw + kw], wk_ref[...]) + nt(own[:, qw + kw :], wv_ref[...])
    ).astype(BF)
    mine = pl.ds(pl.multiple_of(i * db, db), db)
    w_rows = jnp.concatenate([wq_ref[mine], wk_ref[mine], wv_ref[mine]], axis=1).astype(F32)
    gain = jnp.sum(qkvg_ref[:db] * w_rows, axis=1, keepdims=True) / gcol_ref[mine]
    if db < rows:
        gain = jnp.concatenate([gain, jnp.zeros((rows - db, 1), F32)], axis=0)
    dn_ref[:, width : width + LANES] = jnp.broadcast_to(gain, (rows, LANES)).astype(BF)
    dn_ref[:, width + LANES :] = moe_ref[...]


def attend_back(n_exp, pos, q_all, kv_all, do_all, cos, sin, wq, wk, wv, gain_col, moe):
    blocks, _, rows, kw = kv_all.shape
    width, qw = wq.shape
    heads, group = kw // HD, LANES // HD
    n = blocks * rows
    per_head = pltpu.VMEM((heads, group, n, HD), BF)
    return pl.pallas_call(
        functools.partial(attend_back_kernel, n_exp),
        in_specs=[pl.BlockSpec(memory_space=pltpu.SMEM)] + [pl.BlockSpec()] * 10,
        out_shape=[
            jax.ShapeDtypeStruct((rows, 2 * width + LANES), BF),
            jax.ShapeDtypeStruct((LANES, qw + 2 * kw), F32),
            jax.ShapeDtypeStruct((qw, LANES), F32),
            jax.ShapeDtypeStruct((width // LANES, LANES), F32),
        ],
        scratch_shapes=[
            per_head,
            pltpu.VMEM((heads, n, HD), BF),
            pltpu.VMEM((heads, n, HD), BF),
            per_head,
            pltpu.VMEM((heads, group, n, HD), F32),
            pltpu.VMEM((heads, HD, n), F32),
            pltpu.VMEM((heads, HD, n), F32),
            pltpu.VMEM((blocks, rows, qw + 2 * kw), BF),
            per_head,
            pltpu.VMEM((n, qw), BF),
        ],
        compiler_params=params(),
        cost_estimate=cost(18),
        name="attend_back",
    )(pos, q_all, kv_all, do_all, cos, sin, wq, wk, wv, gain_col, moe)


def experts_all_kernel(n_sh, rows, n_exp, *refs):
    pos_ref, refs = refs[0], refs[1:]
    xs, ogs = refs[:n_sh], refs[n_sh : 2 * n_sh]
    small_ref = refs[2 * n_sh]
    base = 2 * n_sh + 1
    wgs, wus, wds = (refs[base + k * n_sh : base + (k + 1) * n_sh] for k in range(3))
    gg_ref, ug_ref, dg_ref, rg_ref, acc = refs[base + 3 * n_sh :]
    e, c = pl.program_id(0), pl.program_id(1)
    nb = xs[0].shape[0]
    tb = nb * rows
    planes = wgs[0].shape[1] // LANES
    lane = lax.broadcasted_iota(jnp.int32, (tb, LANES), 1)
    mine = lane == pos_ref[1] * pl.num_programs(0) + e
    pad = jnp.zeros((LANES - n_exp, rows), F32)
    gates = [jnp.transpose(jnp.concatenate([xs[0][t, planes * rows :].astype(F32), pad], axis=0)) for t in range(nb)]
    gate = jnp.sum(jnp.where(mine, jnp.concatenate(gates, axis=0), 0.0), axis=-1, keepdims=True)
    x_planes = [[x[:, m * rows : (m + 1) * rows].reshape(tb, LANES) for m in range(planes)] for x in xs]
    block = [pos_ref[3 + c * nb + t] for t in range(nb)]
    o_planes = [[o[:, m].reshape(tb, LANES) for m in range(planes)] for o in ogs]
    xv = [jnp.concatenate(p, axis=1) for p in x_planes]
    ov = [jnp.concatenate(p, axis=1) for p in o_planes]
    pg = sum(nn(x, w[0]) for x, w in zip(xv, wgs))
    pu = sum(nn(x, w[0]) for x, w in zip(xv, wus))
    g_out = sum(nt(o, w[0]) for o, w in zip(ov, wds))
    hid, dpg, dpu = expert_terms(pg, pu, g_out, gate)
    hg = (gate * hid).astype(BF)
    plane = pos_ref[2]
    xc, oc = x_planes[0][0], o_planes[0][0]
    for b in range(n_sh):
        for m in range(planes):
            hit = plane == (pos_ref[1] ^ b) * planes + m
            xc = jnp.where(hit, x_planes[b][m], xc)
            oc = jnp.where(hit, o_planes[b][m], oc)

    @pl.when(e == 0)
    def _():
        part = nn(jnp.concatenate([small_ref[j, :n_exp] for j in block], axis=1), xc)
        part = jnp.concatenate([part, jnp.zeros((LANES - n_exp, LANES), F32)], axis=0)
        part = jnp.transpose(part)[:, :n_exp]

        @pl.when(c == 0)
        def _():
            rg_ref[...] = part

        @pl.when(c > 0)
        def _():
            rg_ref[...] += part

    gg, ug, dg = tn(xc, dpg), tn(xc, dpu), tn(oc, hg)

    @pl.when(c == 0)
    def _():
        gg_ref[0] = gg
        ug_ref[0] = ug
        acc[...] = dg

    @pl.when(c > 0)
    def _():
        gg_ref[0] += gg
        ug_ref[0] += ug
        acc[...] += dg

    @pl.when(c == pl.num_programs(1) - 1)
    def _():
        dg_ref[0] = jnp.transpose(acc[...])


def experts_all(n_exp, pos, xs, ogs, small, wg, wu, wd):
    n_sh = len(xs)
    blocks, total, _ = xs[0].shape
    _, planes, rows, _ = ogs[0].shape
    piece = planes * LANES
    n = blocks * rows
    n_e, width, ff = wg.shape
    nb = math.gcd(blocks, 8)
    x_tok = pl.BlockSpec((nb, total, LANES), lambda e, c, p: (c, 0, 0))
    o_tok = pl.BlockSpec((nb, planes, rows, LANES), lambda e, c, p: (c, 0, 0, 0))
    row_w = lambda b: pl.BlockSpec((1, piece, ff), lambda e, c, p, b=b: (e, p[1] ^ b, 0))
    col_w = lambda b: pl.BlockSpec((1, ff, piece), lambda e, c, p, b=b: (e, 0, p[1] ^ b))
    out = pl.BlockSpec((1, LANES, ff), lambda e, c, p: (e, 0, 0))
    out_t = pl.BlockSpec((1, ff, LANES), lambda e, c, p: (e, 0, 0))
    sh = range(n_sh)
    return pl.pallas_call(
        functools.partial(experts_all_kernel, n_sh, rows, n_exp),
        grid_spec=pltpu.PrefetchScalarGridSpec(
            num_scalar_prefetch=1,
            grid=(n_e, blocks // nb),
            in_specs=[x_tok for _ in sh]
            + [o_tok for _ in sh]
            + [pl.BlockSpec(small.shape, lambda e, c, p: (0, 0, 0))]
            + [row_w(b) for b in sh]
            + [row_w(b) for b in sh]
            + [col_w(b) for b in sh],
            out_specs=[out, out, out_t, pl.BlockSpec((LANES, n_exp), lambda e, c, p: (0, 0))],
            scratch_shapes=[pltpu.VMEM((LANES, ff), F32)],
        ),
        out_shape=[jax.ShapeDtypeStruct((n_e, LANES, ff), F32)] * 2
        + [jax.ShapeDtypeStruct((n_e, ff, LANES), F32), jax.ShapeDtypeStruct((LANES, n_exp), F32)],
        compiler_params=params(("arbitrary", "arbitrary")),
        cost_estimate=cost(25),
        name="experts_all",
    )(pos, *xs, *ogs, small, *[wg] * n_sh, *[wu] * n_sh, *[wd] * n_sh)


def finish_kernel(near_ref, far_ref, x_ref, gain_ref, dmid_ref, resid_ref, out_ref, dgain_ref, block_ref):
    width = x_ref.shape[1]
    total = near_ref[...].astype(F32) + far_ref[...].astype(F32)
    block_ref[...] = resid_ref[...] + total[:, width + LANES :]
    dgain_ref[...] = jnp.transpose(total[:, width : width + LANES])[:8]
    x = x_ref[...].astype(F32)
    inv = lax.rsqrt(jnp.mean(x * x, axis=-1, keepdims=True) + NORM_EPS)
    hat = x * inv
    u = gain_ref[...] * total[:, :width]
    out_ref[...] = dmid_ref[...] + inv * (u - hat * jnp.mean(u * hat, axis=-1, keepdims=True))


def finish(near, far, block_in, gain, d_mid, resid):
    rows, width = block_in.shape
    return pl.pallas_call(
        finish_kernel,
        out_shape=[
            jax.ShapeDtypeStruct((rows, width), F32),
            jax.ShapeDtypeStruct((8, rows), F32),
            jax.ShapeDtypeStruct((rows, width), F32),
        ],
        compiler_params=params(),
        cost_estimate=cost(2),
        name="finish",
    )(near, far, block_in, gain, d_mid, resid)


def exchange(x, bit):
    size = lax.axis_size("shard")
    return lax.ppermute(x, "shard", [(j, j ^ bit) for j in range(size)])


def double_ctx(x, bit):
    size = lax.axis_size("ctx")
    far = lax.ppermute(x, "ctx", [(j, j ^ bit) for j in range(size)])
    return jnp.concatenate([x, far], axis=0)


def ctx_bits():
    count = lax.axis_size("ctx").bit_length() - 1
    return [1 << b for b in reversed(range(count))]


def ctx_order(size):
    order = [0]
    bit = size // 2
    while bit:
        order = order + [o ^ bit for o in order]
        bit //= 2
    return jnp.array(order, jnp.int32) ^ lax.axis_index("ctx")


def swap_ctx(x):
    return lax.all_to_all(x, "ctx", 0, 0, tiled=True)


def gather_shard(x):
    found = {0: x}
    bit = lax.axis_size("shard") // 2
    while bit:
        for off in list(found):
            found[off ^ bit] = exchange(found[off], bit)
        bit //= 2
    return [found[b] for b in range(len(found))]


def halves_shard(x):
    last = lax.axis_size("shard") // 2
    bit = 1
    while bit < last:
        x = (x.astype(F32) + exchange(x, bit).astype(F32)).astype(x.dtype)
        bit *= 2
    return x, exchange(x, last)


def after(x, token):
    return lax.optimization_barrier((x, token))[0]


def body(
    block_in,
    attn_gain,
    q_weight,
    k_weight,
    v_weight,
    o_weight,
    moe_gain,
    router_weight,
    expert_gate,
    expert_up,
    expert_down,
    routes,
    out_grad,
):
    rows, width = block_in.shape
    n_ctx, n_sh = lax.axis_size("ctx"), lax.axis_size("shard")
    seq_len = rows * n_ctx
    n_exp = router_weight.shape[1]
    db = width // n_ctx
    qw, kw = q_weight.shape[1], k_weight.shape[1]
    q_planes = qw // LANES
    i, s = lax.axis_index("ctx"), lax.axis_index("shard")
    lane_at = (i * db) % LANES
    pos = jnp.concatenate([jnp.stack([i, s, (i * db) // LANES]).astype(jnp.int32), ctx_order(n_ctx)])
    cos, sin = rope_constants(seq_len)
    gain_one = attn_gain.reshape(1, width)
    gain_two = moe_gain.reshape(1, width)
    router_pad = jnp.pad(router_weight, ((0, 0), (0, LANES - n_exp)))

    piece = width // n_sh
    bits = ctx_bits()
    og_all = lax.dynamic_slice_in_dim(out_grad, s * piece, piece, 1).astype(BF)
    og_all = og_all.reshape(1, rows, piece // LANES, LANES).swapaxes(1, 2)
    og_all = double_ctx(og_all, bits[0])
    kv_send, aux_send = project(
        pos, n_ctx, block_in, gain_one, q_weight, k_weight, v_weight, cos, sin
    )
    kv_all = swap_ctx(kv_send)
    ow = gather_shard(o_weight)
    kv_all = after(kv_all, (ow, og_all))
    for bit in bits[1:-1]:
        og_all = double_ctx(og_all, bit)
    aux_all = swap_ctx(after(aux_send, kv_all))
    heads = attend(pos, aux_send, kv_all)
    resid_mid, x2, gates, x2_send = mid(
        pos, n_exp, gather_shard(heads), ow, block_in, gain_two, router_pad, routes
    )
    x2 = after(x2, og_all)
    og_all = double_ctx(og_all, bits[-1])
    x2_all = double_ctx(x2_send, bits[0])
    moe_part, ex_part = experts_own(pos, x2, out_grad, gates, expert_gate, expert_up, expert_down)
    near, far = halves_shard(ex_part)
    x2_all = after(x2_all, near)
    for bit in bits[1:-1]:
        x2_all = double_ctx(x2_all, bit)
    d_mid, back_send = back_mid(
        n_ctx, n_exp, near, after(far, (x2_all, og_all)), resid_mid, gain_two, gates, router_pad, out_grad, o_weight
    )
    x2_all = double_ctx(x2_all, bits[-1])
    back_all = swap_ctx(after(back_send, aux_all))
    ogs = gather_shard(og_all)
    xs = gather_shard(x2_all)
    back_all = after(back_all, (ogs[n_sh // 2], x2_all))
    dn_part, qkv_grad, o_grad, moe_gain_sum = attend_back(
        n_exp, pos, aux_all, kv_all, back_all, cos, sin, q_weight, k_weight, v_weight,
        attn_gain.reshape(width, 1), moe_part
    )
    in_grad, gain_sum, block_out = finish(*halves_shard(dn_part), block_in, gain_one, d_mid, resid_mid)
    attn_gain_grad = gain_sum[0, :db]
    q_grad, k_grad, v_grad = qkv_grad[:db, :qw], qkv_grad[:db, qw : qw + kw], qkv_grad[:db, qw + kw :]
    o_grad = o_grad[:, :db]

    small = back_all[:, (q_planes + 1) * rows :]
    gate_grad, up_grad, down_grad, router_grad = experts_all(
        n_exp, pos, xs, ogs, small, expert_gate, expert_up, expert_down
    )
    if db < LANES:
        gate_grad = lax.dynamic_slice_in_dim(gate_grad, lane_at, db, 1)
        up_grad = lax.dynamic_slice_in_dim(up_grad, lane_at, db, 1)
        down_grad = lax.dynamic_slice_in_dim(down_grad, lane_at, db, 2)
        router_grad = lax.dynamic_slice_in_dim(router_grad, lane_at, db, 0)
    moe_gain_grad = lax.dynamic_slice_in_dim(moe_gain_sum.reshape(width), i * db, db, 0)
    return (
        block_out,
        in_grad,
        attn_gain_grad,
        q_grad,
        k_grad,
        v_grad,
        o_grad,
        moe_gain_grad,
        router_grad,
        gate_grad,
        up_grad,
        down_grad,
    )


def solution(mesh):
    in_specs = (
        P("ctx", None),
        P(),
        P(None, "shard"),
        P(None, "shard"),
        P(None, "shard"),
        P("shard", None),
        P(),
        P(),
        P("shard", None, None),
        P("shard", None, None),
        P("shard", None, None),
        P("ctx", None),
        P("ctx", None),
    )
    out_specs = (
        P("ctx", None),
        P("ctx", None),
        P("ctx"),
        P("ctx", "shard"),
        P("ctx", "shard"),
        P("ctx", "shard"),
        P("shard", "ctx"),
        P("ctx"),
        P("ctx", None),
        P("shard", "ctx", None),
        P("shard", "ctx", None),
        P("shard", None, "ctx"),
    )
    return jax.shard_map(body, mesh=mesh, in_specs=in_specs, out_specs=out_specs, check_vma=False)
```

```python
import functools
import math

import jax
import jax.numpy as jnp
import numpy as np
from jax import lax
from jax.experimental import pallas as pl
from jax.experimental.pallas import tpu as pltpu
from jax.sharding import PartitionSpec as P

HD = 64
NORM_EPS = 1e-06
ROPE_BASE = 10000.0
BF = jnp.bfloat16
F32 = jnp.float32
LANES = 128
COST = 0.05
VMEM_LIMIT = 56 * 1024 * 1024


def nn(a, b):
    return lax.dot_general(a, b, (((1,), (0,)), ((), ())), preferred_element_type=F32)


def nt(a, b):
    return lax.dot_general(a, b, (((1,), (1,)), ((), ())), preferred_element_type=F32)


def tn(a, b):
    return lax.dot_general(a, b, (((0,), (0,)), ((), ())), preferred_element_type=F32)


def rope_constants(seq_len):
    half = HD // 2
    steps = np.arange(half, dtype=np.float32) * np.float32(2.0 / HD)
    inv_freq = np.exp(np.float32(-math.log(ROPE_BASE)) * steps).astype(np.float32)
    angles = np.arange(seq_len, dtype=np.float32)[:, None] * inv_freq[None, :]
    cos, sin = np.cos(angles), np.sin(angles)
    cos_tab = np.concatenate([cos, cos, cos, cos], axis=1)
    sin_tab = np.concatenate([-sin, sin, -sin, sin], axis=1)
    return jnp.asarray(cos_tab, F32), jnp.asarray(sin_tab, F32)


def swap_halves(vals):
    width = vals.shape[-1]
    lane = lax.broadcasted_iota(jnp.int32, vals.shape, 1)
    up = pltpu.roll(vals, width - HD // 2, 1)
    down = pltpu.roll(vals, HD // 2, 1)
    return jnp.where(lane % HD < HD // 2, up, down)


def widen(tab, width):
    reps = width // tab.shape[1]
    return tab if reps == 1 else jnp.concatenate([tab] * reps, axis=1)


def rope(vals, cos, sin):
    width = vals.shape[-1]
    return vals * widen(cos, width) + swap_halves(vals) * widen(sin, width)


def unrope(vals, cos, sin):
    width = vals.shape[-1]
    return vals * widen(cos, width) - swap_halves(vals) * widen(sin, width)


def params(semantics=None):
    return pltpu.CompilerParams(dimension_semantics=semantics, vmem_limit_bytes=VMEM_LIMIT)


def cost(micros):
    return pl.CostEstimate(flops=0, transcendentals=0, bytes_accessed=int(micros * COST * 3.69e6))


def project_kernel(pos_ref, x_ref, gain_ref, wq_ref, wk_ref, wv_ref, cos_ref, sin_ref, kv_ref, aux_ref):
    x = x_ref[...].astype(F32)
    inv = lax.rsqrt(jnp.mean(x * x, axis=-1, keepdims=True) + NORM_EPS)
    x1 = (x * inv * gain_ref[...]).astype(BF)
    cos, sin = cos_ref[...], sin_ref[...]
    q = rope(nn(x1, wq_ref[...]), cos, sin).astype(BF)
    q = (q.astype(F32) * (HD**-0.5)).astype(BF)
    k = rope(nn(x1, wk_ref[...]), cos, sin).astype(BF)
    v = nn(x1, wv_ref[...]).astype(BF)
    peers, _, rows, _ = aux_ref.shape
    aux = [q[:, m * LANES : (m + 1) * LANES] for m in range(q.shape[1] // LANES)]
    db = x.shape[1] // peers
    for p in range(peers):
        kv_ref[p, 0] = k
        kv_ref[p, 1] = v
        for m in range(len(aux)):
            aux_ref[p, m] = aux[m]
        cols = x1[:, p * db : (p + 1) * db]
        if db < LANES:
            cols = jnp.concatenate([cols, jnp.zeros((rows, LANES - db), BF)], axis=1)
        aux_ref[p, len(aux)] = cols


def project(pos, peers, block_in, gain, wq, wk, wv, cos, sin):
    rows, width = block_in.shape
    planes = wq.shape[1] // LANES + 1
    full = lambda shape: pl.BlockSpec(shape, lambda g, p: (0,) * len(shape))
    tab = pl.BlockSpec((rows, LANES), lambda g, p: (p[0], 0))
    return pl.pallas_call(
        project_kernel,
        grid_spec=pltpu.PrefetchScalarGridSpec(
            num_scalar_prefetch=1,
            grid=(1,),
            in_specs=[
                full((rows, width)),
                full((1, width)),
                full(wq.shape),
                full(wk.shape),
                full(wv.shape),
                tab,
                tab,
            ],
            out_specs=[full((peers, 2, rows, LANES)), full((peers, planes, rows, LANES))],
        ),
        out_shape=[
            jax.ShapeDtypeStruct((peers, 2, rows, LANES), BF),
            jax.ShapeDtypeStruct((peers, planes, rows, LANES), BF),
        ],
        compiler_params=params(),
        cost_estimate=cost(3),
        name="project",
    )(pos, block_in, gain, wq, wk, wv, cos, sin)


def attend_kernel(pos_ref, q_ref, kv_ref, out_ref):
    i = pos_ref[0]
    blocks, _, rows, kw = kv_ref.shape
    heads = kw // HD
    group = q_ref.shape[2] // HD
    n = blocks * rows
    k_all = kv_ref[:, 0].reshape(n, kw)
    v_all = kv_ref[:, 1].reshape(n, kw)
    col = lax.broadcasted_iota(jnp.int32, (group * rows, n), 1)
    row = lax.broadcasted_iota(jnp.int32, (group * rows, n), 0) % rows + i * rows
    allowed = col <= row
    for h in range(heads):
        k = k_all[:, h * HD : (h + 1) * HD]
        v = v_all[:, h * HD : (h + 1) * HD]
        q = jnp.concatenate([q_ref[h, :, g * HD : (g + 1) * HD] for g in range(group)], axis=0)
        s = jnp.where(allowed, nt(q, k), -1e30)
        top = jnp.max(s, axis=-1, keepdims=True)
        e = jnp.exp(s - top)
        total = jnp.sum(e, axis=-1, keepdims=True)
        o = (nn(e.astype(BF), v) / total).astype(BF)
        for g in range(group):
            c = (h * group + g) * HD
            out_ref[:, c : c + HD] = o[g * rows : (g + 1) * rows]


def attend(pos, aux, kv_all):
    _, _, rows, _ = aux.shape
    q_planes = kv_all.shape[3] // HD
    return pl.pallas_call(
        attend_kernel,
        grid_spec=pltpu.PrefetchScalarGridSpec(
            num_scalar_prefetch=1,
            grid=(1,),
            in_specs=[
                pl.BlockSpec((None, q_planes, rows, LANES), lambda g, p: (0, 0, 0, 0)),
                pl.BlockSpec(kv_all.shape, lambda g, p: (0, 0, 0, 0)),
            ],
            out_specs=pl.BlockSpec((rows, q_planes * LANES), lambda g, p: (0, 0)),
        ),
        out_shape=jax.ShapeDtypeStruct((rows, q_planes * LANES), BF),
        compiler_params=params(),
        cost_estimate=cost(3),
        name="attend",
    )(pos, aux, kv_all)


def mid_kernel(n_sh, *refs):
    pos_ref = refs[0]
    heads = refs[1 : n_sh + 1]
    ow = refs[n_sh + 1 : 2 * n_sh + 1]
    x_ref, gain_ref, router_ref, routes_ref, resid_ref, x2_ref, gates_ref, send_ref = refs[2 * n_sh + 1 :]
    acc = x_ref[...].astype(F32)
    for h, w in zip(heads, ow):
        acc = acc + nn(h[...], w[...])
    resid_ref[...] = acc
    inv = lax.rsqrt(jnp.mean(acc * acc, axis=-1, keepdims=True) + NORM_EPS)
    x2 = (acc * inv * gain_ref[...]).astype(BF)
    x2_ref[...] = x2
    logits = nn(x2, router_ref[...])
    lane = lax.broadcasted_iota(jnp.int32, logits.shape, 1)
    chosen = lane < 0
    for k in range(routes_ref.shape[1]):
        chosen = chosen | (routes_ref[:, k : k + 1] == lane)
    masked = jnp.where(chosen, logits, -1e30)
    e = jnp.where(chosen, jnp.exp(masked - jnp.max(masked, axis=-1, keepdims=True)), 0.0)
    gates = e / jnp.sum(e, axis=-1, keepdims=True)
    gates_ref[...] = gates
    rows, width = acc.shape
    planes = width // n_sh // LANES
    n_gate = send_ref.shape[1] - planes * rows
    g_rows = jnp.transpose(gates)[:n_gate].astype(BF)
    s = pos_ref[1]
    mine = []
    for m in range(planes):
        plane = x2[:, m * LANES : (m + 1) * LANES]
        for k in range(1, n_sh):
            at = (k * planes + m) * LANES
            plane = jnp.where(s == k, x2[:, at : at + LANES], plane)
        mine.append(plane)
    for m in range(planes):
        send_ref[0, m * rows : (m + 1) * rows] = mine[m]
    send_ref[0, planes * rows :] = g_rows


def mid(pos, n_gate, heads, ow, block_in, gain, router_pad, routes):
    rows, width = block_in.shape
    n_sh = len(heads)
    total = width // n_sh // LANES * rows + n_gate
    return pl.pallas_call(
        functools.partial(mid_kernel, n_sh),
        in_specs=[pl.BlockSpec(memory_space=pltpu.SMEM)] + [pl.BlockSpec()] * (2 * n_sh + 4),
        out_shape=[
            jax.ShapeDtypeStruct((rows, width), F32),
            jax.ShapeDtypeStruct((rows, width), BF),
            jax.ShapeDtypeStruct((rows, LANES), F32),
            jax.ShapeDtypeStruct((1, total, LANES), BF),
        ],
        compiler_params=params(),
        cost_estimate=cost(4),
        name="mid",
    )(pos, *heads, *ow, block_in, gain, router_pad, routes)


def expert_terms(pg, pu, g_out, gate):
    sig = 0.5 + 0.5 * jnp.tanh(0.5 * pg)
    silu = pg * sig
    hid = silu * pu
    dh = gate * g_out
    dpg = (dh * pu * (sig * (1.0 + pg * (1.0 - sig)))).astype(BF)
    dpu = (dh * silu).astype(BF)
    return hid, dpg, dpu


def experts_own_kernel(pos_ref, x_ref, og_ref, gates_ref, wg_ref, wu_ref, wd_ref, moe_ref, ex_ref, acc_m, acc_d, acc_g):
    e = pl.program_id(0)
    n_e = pl.num_programs(0)
    width = x_ref.shape[1]

    @pl.when(e == 0)
    def _():
        acc_m[...] = jnp.zeros_like(acc_m)
        acc_d[...] = jnp.zeros_like(acc_d)
        acc_g[...] = jnp.zeros_like(acc_g)

    lane = lax.broadcasted_iota(jnp.int32, gates_ref.shape, 1)
    mine = lane == pos_ref[1] * n_e + e
    gate = jnp.sum(jnp.where(mine, gates_ref[...], 0.0), axis=-1, keepdims=True)
    x = x_ref[...]
    wg, wu, wd = wg_ref[0], wu_ref[0], wd_ref[0]
    pg, pu, g_out = nn(x, wg), nn(x, wu), nt(og_ref[...].astype(BF), wd)
    hid, dpg, dpu = expert_terms(pg, pu, g_out, gate)
    d_gate = jnp.sum(hid.astype(BF).astype(F32) * g_out, axis=-1, keepdims=True)
    acc_m[...] += nn((gate * hid).astype(BF), wd)
    acc_d[...] += nt(dpg, wg) + nt(dpu, wu)
    acc_g[...] += jnp.where(mine, d_gate, 0.0)

    @pl.when(e == n_e - 1)
    def _():
        moe_ref[...] = acc_m[...].astype(BF)
        ex_ref[:, :width] = acc_d[...].astype(BF)
        ex_ref[:, width:] = acc_g[...].astype(BF)


def experts_own(pos, x2, og, gates, wg, wu, wd):
    rows, width = x2.shape
    n_e, _, ff = wg.shape
    full = lambda shape: pl.BlockSpec(shape, lambda e, p: (0,) * len(shape))
    return pl.pallas_call(
        experts_own_kernel,
        grid_spec=pltpu.PrefetchScalarGridSpec(
            num_scalar_prefetch=1,
            grid=(n_e,),
            in_specs=[
                full((rows, width)),
                full((rows, width)),
                full((rows, LANES)),
                pl.BlockSpec((1, width, ff), lambda e, p: (e, 0, 0)),
                pl.BlockSpec((1, width, ff), lambda e, p: (e, 0, 0)),
                pl.BlockSpec((1, ff, width), lambda e, p: (e, 0, 0)),
            ],
            out_specs=[full((rows, width)), full((rows, width + LANES))],
            scratch_shapes=[
                pltpu.VMEM((rows, width), F32),
                pltpu.VMEM((rows, width), F32),
                pltpu.VMEM((rows, LANES), F32),
            ],
        ),
        out_shape=[
            jax.ShapeDtypeStruct((rows, width), BF),
            jax.ShapeDtypeStruct((rows, width + LANES), BF),
        ],
        compiler_params=params(("arbitrary",)),
        cost_estimate=cost(11),
        name="experts_own",
    )(pos, x2, og, gates, wg, wu, wd)


def back_mid_kernel(
    n_exp, ex_ref, far_ref, resid_ref, gain_ref, gates_ref, router_ref, og_ref, ow_ref, dmid_ref, send_ref
):
    rows, width = resid_ref.shape
    ex = ex_ref[...].astype(F32) + far_ref[...].astype(F32)
    gates = gates_ref[...]
    d_gate = ex[:, width:]
    d_logits = gates * (d_gate - jnp.sum(gates * d_gate, axis=-1, keepdims=True))
    d_norm = ex[:, :width] + nt(d_logits.astype(BF), router_ref[...])
    resid = resid_ref[...]
    inv = lax.rsqrt(jnp.mean(resid * resid, axis=-1, keepdims=True) + NORM_EPS)
    hat = resid * inv
    d_gain = jnp.sum(d_norm * hat, axis=0, keepdims=True)
    u = gain_ref[...] * d_norm
    inner = jnp.mean(u * hat, axis=-1, keepdims=True)
    d_mid = og_ref[...] + inv * (u - hat * inner)
    dmid_ref[...] = d_mid
    dmb = d_mid.astype(BF)
    d_heads = nt(dmb, ow_ref[...]).astype(BF)
    planes = d_heads.shape[1] // LANES
    gain_rows = [d_gain[:, k * LANES : (k + 1) * LANES] for k in range(width // LANES)]
    small = jnp.concatenate([jnp.transpose(d_logits)[:n_exp]] + gain_rows, axis=0).astype(BF)
    peers = send_ref.shape[0]
    db = width // peers
    for p in range(peers):
        for m in range(planes):
            send_ref[p, m * rows : (m + 1) * rows] = d_heads[:, m * LANES : (m + 1) * LANES]
        cols = dmb[:, p * db : (p + 1) * db]
        if db < LANES:
            cols = jnp.concatenate([cols, jnp.zeros((rows, LANES - db), BF)], axis=1)
        send_ref[p, planes * rows : (planes + 1) * rows] = cols
        send_ref[p, (planes + 1) * rows :] = small


def back_mid(peers, n_exp, ex, far, resid, gain, gates, router_pad, og, ow):
    rows, width = resid.shape
    total = (ow.shape[0] // LANES + 1) * rows + n_exp + width // LANES
    return pl.pallas_call(
        functools.partial(back_mid_kernel, n_exp),
        out_shape=[
            jax.ShapeDtypeStruct((rows, width), F32),
            jax.ShapeDtypeStruct((peers, total, LANES), BF),
        ],
        compiler_params=params(),
        cost_estimate=cost(3),
        name="back_mid",
    )(ex, far, resid, gain, gates, router_pad, og, ow)


def block_probs(q, k, start, first, bq):
    s = nt(q, k)
    edge = s[:, first:]
    col = lax.broadcasted_iota(jnp.int32, edge.shape, 1) + first
    row = lax.broadcasted_iota(jnp.int32, edge.shape, 0) % bq + start
    edge = jnp.where(col <= row, edge, -1e30)
    s = edge if first == 0 else jnp.concatenate([s[:, :first], edge], axis=1)
    e = jnp.exp(s - jnp.max(s, axis=-1, keepdims=True))
    return e, 1.0 / jnp.sum(e, axis=-1, keepdims=True)


def load_heads(dst, block, j, h):
    rows = block.shape[0]
    for g in range(LANES // HD):
        dst[h, g, j * rows : (j + 1) * rows] = block[:, g * HD : (g + 1) * HD]


def load_keys(ks, vs, kv_ref):
    blocks, _, rows, kw = kv_ref.shape
    for j in range(blocks):
        for h in range(kw // HD):
            ks[h, j * rows : (j + 1) * rows] = kv_ref[j, 0, :, h * HD : (h + 1) * HD]
            vs[h, j * rows : (j + 1) * rows] = kv_ref[j, 1, :, h * HD : (h + 1) * HD]


def stacked(src, h, start, bq):
    return jnp.concatenate([src[h, g, pl.ds(start, bq)] for g in range(LANES // HD)], axis=0)


def attend_back_kernel(n_exp, *refs):
    pos_ref, q_ref, kv_ref, do_ref, cos_ref, sin_ref, wq_ref, wk_ref, wv_ref, gcol_ref, moe_ref = refs[:11]
    dn_ref, qg_ref, kg_ref, vg_ref, og_ref, mg_ref, qs, ks, vs, dos, dqs, dkt, dvt, dqkv, hos, hfull = refs[11:]
    i = pos_ref[0]
    blocks, _, rows, kw = kv_ref.shape
    heads = kw // HD
    group = LANES // HD
    qw = heads * LANES
    n = blocks * rows
    bq = 4 * rows if n <= 1024 else rows // 2
    load_keys(ks, vs, kv_ref)
    for j in range(blocks):
        for h in range(heads):
            load_heads(qs, q_ref[j, h], j, h)
            load_heads(dos, do_ref[j, h * rows : (h + 1) * rows], j, h)
    dkt[...] = jnp.zeros_like(dkt)
    dvt[...] = jnp.zeros_like(dvt)

    def step(h, start, ext, first):
        k, v = ks[h, :ext], vs[h, :ext]
        q, do = stacked(qs, h, start, bq), stacked(dos, h, start, bq)
        e, inv = block_probs(q, k, start, first, bq)
        p = e * inv
        pb = p.astype(BF)
        o = nn(pb, v).astype(BF)
        delta = jnp.sum(do.astype(F32) * o.astype(F32), axis=-1, keepdims=True)
        ds = (p * (nt(do, v) - delta)).astype(BF)
        dq = nn(ds, k) * (HD**-0.5)
        dkt[h, :, :ext] += tn(q, ds)
        dvt[h, :, :ext] += tn(do, pb)
        for g in range(group):
            dqs[h, g, pl.ds(start, bq)] = dq[g * bq : (g + 1) * bq]
            hos[h, g, pl.ds(start, bq)] = o[g * bq : (g + 1) * bq]

    def per_head(h, carry):
        if n <= 1024:
            for r in range(n // bq):
                step(h, r * bq, (r + 1) * bq, r * bq)
        else:

            def loop(r, c):
                step(h, pl.multiple_of(r * bq, bq), n, 0)
                return c

            lax.fori_loop(0, n // bq, loop, 0)
        return carry

    lax.fori_loop(0, heads, per_head, 0)
    pieces = [(h, g) for h in range(heads) for g in range(group)]
    small = (heads + 1) * rows
    gain_rows = jnp.sum(do_ref[:, small + n_exp :].astype(F32), axis=0)
    mine = lax.broadcasted_iota(jnp.int32, gain_rows.shape, 0) == pos_ref[2]
    mg_ref[...] = jnp.sum(jnp.where(mine, gain_rows, 0.0), axis=0, keepdims=True)

    def per_block(j, carry):
        at = pl.ds(pl.multiple_of(j * rows, rows), rows)
        cos, sin = cos_ref[at], sin_ref[at]
        hfull[at] = jnp.concatenate([hos[h, g, at] for h, g in pieces], axis=1)
        dq = jnp.concatenate([dqs[h, g, at] for h, g in pieces], axis=1)
        dk = jnp.transpose(jnp.concatenate([dkt[h, :, at] for h in range(heads)], axis=0))
        dv = jnp.transpose(jnp.concatenate([dvt[h, :, at] for h in range(heads)], axis=0))
        out = jnp.concatenate([unrope(dq, cos, sin), unrope(dk, cos, sin), dv], axis=1).astype(BF)
        dqkv[j] = out
        return carry

    lax.fori_loop(0, blocks, per_block, 0, unroll=2)
    qkvg = tn(q_ref[:, q_ref.shape[1] - 1].reshape(n, LANES), dqkv[...].reshape(n, qw + 2 * kw))
    qg_ref[...] = qkvg[:, :qw]
    kg_ref[...] = qkvg[:, qw : qw + kw]
    vg_ref[...] = qkvg[:, qw + kw :]
    og_ref[...] = tn(hfull[...], do_ref[:, heads * rows : (heads + 1) * rows].reshape(n, LANES))
    own = dqkv[i]
    width = wq_ref.shape[0]
    db = width // blocks
    dn_ref[:, :width] = (
        nt(own[:, :qw], wq_ref[...]) + nt(own[:, qw : qw + kw], wk_ref[...]) + nt(own[:, qw + kw :], wv_ref[...])
    ).astype(BF)
    mine = pl.ds(pl.multiple_of(i * db, db), db)
    w_rows = jnp.concatenate([wq_ref[mine], wk_ref[mine], wv_ref[mine]], axis=1).astype(F32)
    gain = jnp.sum(qkvg[:db] * w_rows, axis=1, keepdims=True) / gcol_ref[mine]
    if db < rows:
        gain = jnp.concatenate([gain, jnp.zeros((rows - db, 1), F32)], axis=0)
    dn_ref[:, width : width + LANES] = jnp.broadcast_to(gain, (rows, LANES)).astype(BF)
    dn_ref[:, width + LANES :] = moe_ref[...]


def attend_back(n_exp, pos, q_all, kv_all, do_all, cos, sin, wq, wk, wv, gain_col, moe):
    blocks, _, rows, kw = kv_all.shape
    width, qw = wq.shape
    heads, group = kw // HD, LANES // HD
    n = blocks * rows
    per_head = pltpu.VMEM((heads, group, n, HD), BF)
    return pl.pallas_call(
        functools.partial(attend_back_kernel, n_exp),
        in_specs=[pl.BlockSpec(memory_space=pltpu.SMEM)] + [pl.BlockSpec()] * 10,
        out_shape=[
            jax.ShapeDtypeStruct((rows, 2 * width + LANES), BF),
            jax.ShapeDtypeStruct((LANES, qw), F32),
            jax.ShapeDtypeStruct((LANES, kw), F32),
            jax.ShapeDtypeStruct((LANES, kw), F32),
            jax.ShapeDtypeStruct((qw, LANES), F32),
            jax.ShapeDtypeStruct((1, LANES), F32),
        ],
        scratch_shapes=[
            per_head,
            pltpu.VMEM((heads, n, HD), BF),
            pltpu.VMEM((heads, n, HD), BF),
            per_head,
            pltpu.VMEM((heads, group, n, HD), F32),
            pltpu.VMEM((heads, HD, n), F32),
            pltpu.VMEM((heads, HD, n), F32),
            pltpu.VMEM((blocks, rows, qw + 2 * kw), BF),
            per_head,
            pltpu.VMEM((n, qw), BF),
        ],
        compiler_params=params(),
        cost_estimate=cost(18),
        name="attend_back",
    )(pos, q_all, kv_all, do_all, cos, sin, wq, wk, wv, gain_col, moe)


def experts_all_kernel(n_sh, rows, n_exp, *refs):
    pos_ref, refs = refs[0], refs[1:]
    xs, ogs = refs[:n_sh], refs[n_sh : 2 * n_sh]
    small_ref = refs[2 * n_sh]
    base = 2 * n_sh + 1
    wgs, wus, wds = (refs[base + k * n_sh : base + (k + 1) * n_sh] for k in range(3))
    gg_ref, ug_ref, dg_ref, rg_ref, acc = refs[base + 3 * n_sh :]
    e, c = pl.program_id(0), pl.program_id(1)
    nb = xs[0].shape[0]
    tb = nb * rows
    planes = wgs[0].shape[1] // LANES
    lane = lax.broadcasted_iota(jnp.int32, (tb, LANES), 1)
    mine = lane == pos_ref[1] * pl.num_programs(0) + e
    pad = jnp.zeros((LANES - n_exp, rows), F32)
    gates = [jnp.transpose(jnp.concatenate([xs[0][t, planes * rows :].astype(F32), pad], axis=0)) for t in range(nb)]
    gate = jnp.sum(jnp.where(mine, jnp.concatenate(gates, axis=0), 0.0), axis=-1, keepdims=True)
    x_planes = [[x[:, m * rows : (m + 1) * rows].reshape(tb, LANES) for m in range(planes)] for x in xs]
    block = [pos_ref[3 + c * nb + t] for t in range(nb)]
    o_planes = [[o[:, m].reshape(tb, LANES) for m in range(planes)] for o in ogs]
    xv = [jnp.concatenate(p, axis=1) for p in x_planes]
    ov = [jnp.concatenate(p, axis=1) for p in o_planes]
    pg = sum(nn(x, w[0]) for x, w in zip(xv, wgs))
    pu = sum(nn(x, w[0]) for x, w in zip(xv, wus))
    g_out = sum(nt(o, w[0]) for o, w in zip(ov, wds))
    hid, dpg, dpu = expert_terms(pg, pu, g_out, gate)
    hg = (gate * hid).astype(BF)
    plane = pos_ref[2]
    xc, oc = x_planes[0][0], o_planes[0][0]
    for b in range(n_sh):
        for m in range(planes):
            hit = plane == (pos_ref[1] ^ b) * planes + m
            xc = jnp.where(hit, x_planes[b][m], xc)
            oc = jnp.where(hit, o_planes[b][m], oc)

    @pl.when(e == 0)
    def _():
        part = nn(jnp.concatenate([small_ref[j, :n_exp] for j in block], axis=1), xc)

        @pl.when(c == 0)
        def _():
            rg_ref[...] = part

        @pl.when(c > 0)
        def _():
            rg_ref[...] += part

    gg, ug, dg = tn(xc, dpg), tn(xc, dpu), tn(oc, hg)

    @pl.when(c == 0)
    def _():
        gg_ref[0] = gg
        ug_ref[0] = ug
        acc[...] = dg

    @pl.when(c > 0)
    def _():
        gg_ref[0] += gg
        ug_ref[0] += ug
        acc[...] += dg

    @pl.when(c == pl.num_programs(1) - 1)
    def _():
        dg_ref[0] = jnp.transpose(acc[...])


def experts_all(n_exp, pos, xs, ogs, small, wg, wu, wd):
    n_sh = len(xs)
    blocks, total, _ = xs[0].shape
    _, planes, rows, _ = ogs[0].shape
    piece = planes * LANES
    n = blocks * rows
    n_e, width, ff = wg.shape
    nb = math.gcd(blocks, 8)
    tail = small.shape[1] % rows
    x_tok = pl.BlockSpec((nb, total, LANES), lambda e, c, p: (c, 0, 0))
    o_tok = pl.BlockSpec((nb, planes, rows, LANES), lambda e, c, p: (c, 0, 0, 0))
    row_w = lambda b: pl.BlockSpec((1, piece, ff), lambda e, c, p, b=b: (e, p[1] ^ b, 0))
    col_w = lambda b: pl.BlockSpec((1, ff, piece), lambda e, c, p, b=b: (e, 0, p[1] ^ b))
    out = pl.BlockSpec((1, LANES, ff), lambda e, c, p: (e, 0, 0))
    out_t = pl.BlockSpec((1, ff, LANES), lambda e, c, p: (e, 0, 0))
    sh = range(n_sh)
    return pl.pallas_call(
        functools.partial(experts_all_kernel, n_sh, rows, n_exp),
        grid_spec=pltpu.PrefetchScalarGridSpec(
            num_scalar_prefetch=1,
            grid=(n_e, blocks // nb),
            in_specs=[x_tok for _ in sh]
            + [o_tok for _ in sh]
            + [pl.BlockSpec((blocks, tail, LANES), lambda e, c, p: (0, small.shape[1] // tail - 1, 0))]
            + [row_w(b) for b in sh]
            + [row_w(b) for b in sh]
            + [col_w(b) for b in sh],
            out_specs=[out, out, out_t, pl.BlockSpec((n_exp, LANES), lambda e, c, p: (0, 0))],
            scratch_shapes=[pltpu.VMEM((LANES, ff), F32)],
        ),
        out_shape=[jax.ShapeDtypeStruct((n_e, LANES, ff), F32)] * 2
        + [jax.ShapeDtypeStruct((n_e, ff, LANES), F32), jax.ShapeDtypeStruct((n_exp, LANES), F32)],
        compiler_params=params(("arbitrary", "arbitrary")),
        cost_estimate=cost(25),
        name="experts_all",
    )(pos, *xs, *ogs, small, *[wg] * n_sh, *[wu] * n_sh, *[wd] * n_sh)


def finish_kernel(near_ref, far_ref, x_ref, gain_ref, dmid_ref, resid_ref, out_ref, dgain_ref, block_ref):
    width = x_ref.shape[1]
    total = near_ref[...].astype(F32) + far_ref[...].astype(F32)
    block_ref[...] = resid_ref[...] + total[:, width + LANES :]
    dgain_ref[...] = jnp.transpose(total[:, width : width + LANES])[:1]
    x = x_ref[...].astype(F32)
    inv = lax.rsqrt(jnp.mean(x * x, axis=-1, keepdims=True) + NORM_EPS)
    hat = x * inv
    u = gain_ref[...] * total[:, :width]
    out_ref[...] = dmid_ref[...] + inv * (u - hat * jnp.mean(u * hat, axis=-1, keepdims=True))


def finish(near, far, block_in, gain, d_mid, resid):
    rows, width = block_in.shape
    return pl.pallas_call(
        finish_kernel,
        out_shape=[
            jax.ShapeDtypeStruct((rows, width), F32),
            jax.ShapeDtypeStruct((1, rows), F32),
            jax.ShapeDtypeStruct((rows, width), F32),
        ],
        compiler_params=params(),
        cost_estimate=cost(2),
        name="finish",
    )(near, far, block_in, gain, d_mid, resid)


def exchange(x, bit):
    size = lax.axis_size("shard")
    return lax.ppermute(x, "shard", [(j, j ^ bit) for j in range(size)])


def double_ctx(x, bit):
    size = lax.axis_size("ctx")
    far = lax.ppermute(x, "ctx", [(j, j ^ bit) for j in range(size)])
    return jnp.concatenate([x, far], axis=0)


def ctx_bits():
    count = lax.axis_size("ctx").bit_length() - 1
    return [1 << b for b in reversed(range(count))]


def ctx_order(size):
    order = [0]
    bit = size // 2
    while bit:
        order = order + [o ^ bit for o in order]
        bit //= 2
    return jnp.array(order, jnp.int32) ^ lax.axis_index("ctx")


def swap_ctx(x):
    return lax.all_to_all(x, "ctx", 0, 0, tiled=True)


def gather_shard(x):
    found = {0: x}
    bit = lax.axis_size("shard") // 2
    while bit:
        for off in list(found):
            found[off ^ bit] = exchange(found[off], bit)
        bit //= 2
    return [found[b] for b in range(len(found))]


def halves_shard(x):
    last = lax.axis_size("shard") // 2
    bit = 1
    while bit < last:
        x = (x.astype(F32) + exchange(x, bit).astype(F32)).astype(x.dtype)
        bit *= 2
    return x, exchange(x, last)


def after(x, token):
    return lax.optimization_barrier((x, token))[0]


def body(
    block_in,
    attn_gain,
    q_weight,
    k_weight,
    v_weight,
    o_weight,
    moe_gain,
    router_weight,
    expert_gate,
    expert_up,
    expert_down,
    routes,
    out_grad,
):
    rows, width = block_in.shape
    n_ctx, n_sh = lax.axis_size("ctx"), lax.axis_size("shard")
    seq_len = rows * n_ctx
    n_exp = router_weight.shape[1]
    db = width // n_ctx
    qw, kw = q_weight.shape[1], k_weight.shape[1]
    q_planes = qw // LANES
    i, s = lax.axis_index("ctx"), lax.axis_index("shard")
    lane_at = (i * db) % LANES
    pos = jnp.concatenate([jnp.stack([i, s, (i * db) // LANES]).astype(jnp.int32), ctx_order(n_ctx)])
    cos, sin = rope_constants(seq_len)
    gain_one = attn_gain.reshape(1, width)
    gain_two = moe_gain.reshape(1, width)
    router_pad = jnp.pad(router_weight, ((0, 0), (0, LANES - n_exp)))

    piece = width // n_sh
    bits = ctx_bits()
    og_all = lax.dynamic_slice_in_dim(out_grad, s * piece, piece, 1).astype(BF)
    og_all = og_all.reshape(1, rows, piece // LANES, LANES).swapaxes(1, 2)
    og_all = double_ctx(og_all, bits[0])
    kv_send, aux_send = project(
        pos, n_ctx, block_in, gain_one, q_weight, k_weight, v_weight, cos, sin
    )
    kv_all = swap_ctx(kv_send)
    ow = gather_shard(o_weight)
    kv_all = after(kv_all, (ow, og_all))
    for bit in bits[1:-1]:
        og_all = double_ctx(og_all, bit)
    aux_all = swap_ctx(after(aux_send, kv_all))
    heads = attend(pos, aux_send, kv_all)
    resid_mid, x2, gates, x2_send = mid(
        pos, n_exp, gather_shard(heads), ow, block_in, gain_two, router_pad, routes
    )
    x2 = after(x2, og_all)
    og_all = double_ctx(og_all, bits[-1])
    x2_all = double_ctx(x2_send, bits[0])
    moe_part, ex_part = experts_own(pos, x2, out_grad, gates, expert_gate, expert_up, expert_down)
    near, far = halves_shard(ex_part)
    x2_all = after(x2_all, near)
    for bit in bits[1:-1]:
        x2_all = double_ctx(x2_all, bit)
    d_mid, back_send = back_mid(
        n_ctx, n_exp, near, after(far, (x2_all, og_all)), resid_mid, gain_two, gates, router_pad, out_grad, o_weight
    )
    x2_all = double_ctx(x2_all, bits[-1])
    back_all = swap_ctx(after(back_send, aux_all))
    ogs = gather_shard(og_all)
    xs = gather_shard(x2_all)
    back_all = after(back_all, (ogs[n_sh // 2], x2_all))
    dn_part, q_grad, k_grad, v_grad, o_grad, moe_gain_sum = attend_back(
        n_exp, pos, aux_all, kv_all, back_all, cos, sin, q_weight, k_weight, v_weight,
        attn_gain.reshape(width, 1), moe_part
    )
    in_grad, gain_sum, block_out = finish(*halves_shard(dn_part), block_in, gain_one, d_mid, resid_mid)
    attn_gain_grad = gain_sum.reshape(rows)[:db]
    q_grad, k_grad, v_grad = q_grad[:db], k_grad[:db], v_grad[:db]
    o_grad = o_grad[:, :db]

    gate_grad, up_grad, down_grad, router_t = experts_all(
        n_exp, pos, xs, ogs, back_all, expert_gate, expert_up, expert_down
    )
    if db < LANES:
        gate_grad = lax.dynamic_slice_in_dim(gate_grad, lane_at, db, 1)
        up_grad = lax.dynamic_slice_in_dim(up_grad, lane_at, db, 1)
        down_grad = lax.dynamic_slice_in_dim(down_grad, lane_at, db, 2)
        router_t = lax.dynamic_slice_in_dim(router_t, lane_at, db, 1)
    router_grad = router_t.T
    moe_gain_grad = moe_gain_sum.reshape(LANES)
    if db < LANES:
        moe_gain_grad = lax.dynamic_slice_in_dim(moe_gain_grad, lane_at, db, 0)
    return (
        block_out,
        in_grad,
        attn_gain_grad,
        q_grad,
        k_grad,
        v_grad,
        o_grad,
        moe_gain_grad,
        router_grad,
        gate_grad,
        up_grad,
        down_grad,
    )


def solution(mesh):
    in_specs = (
        P("ctx", None),
        P(),
        P(None, "shard"),
        P(None, "shard"),
        P(None, "shard"),
        P("shard", None),
        P(),
        P(),
        P("shard", None, None),
        P("shard", None, None),
        P("shard", None, None),
        P("ctx", None),
        P("ctx", None),
    )
    out_specs = (
        P("ctx", None),
        P("ctx", None),
        P("ctx"),
        P("ctx", "shard"),
        P("ctx", "shard"),
        P("ctx", "shard"),
        P("shard", "ctx"),
        P("ctx"),
        P("ctx", None),
        P("shard", "ctx", None),
        P("shard", "ctx", None),
        P("shard", None, "ctx"),
    )
    return jax.shard_map(body, mesh=mesh, in_specs=in_specs, out_specs=out_specs, check_vma=False)
```

```python
import functools
import math

import jax
import jax.numpy as jnp
import numpy as np
from jax import lax
from jax.experimental import pallas as pl
from jax.experimental.pallas import tpu as pltpu
from jax.sharding import PartitionSpec as P

HD = 64
NORM_EPS = 1e-06
ROPE_BASE = 10000.0
BF = jnp.bfloat16
F32 = jnp.float32
LANES = 128
COST = 0.05
VMEM_LIMIT = 56 * 1024 * 1024


def nn(a, b):
    return lax.dot_general(a, b, (((1,), (0,)), ((), ())), preferred_element_type=F32)


def nt(a, b):
    return lax.dot_general(a, b, (((1,), (1,)), ((), ())), preferred_element_type=F32)


def tn(a, b):
    return lax.dot_general(a, b, (((0,), (0,)), ((), ())), preferred_element_type=F32)


def rope_constants(seq_len):
    half = HD // 2
    steps = np.arange(half, dtype=np.float32) * np.float32(2.0 / HD)
    inv_freq = np.exp(np.float32(-math.log(ROPE_BASE)) * steps).astype(np.float32)
    angles = np.arange(seq_len, dtype=np.float32)[:, None] * inv_freq[None, :]
    cos, sin = np.cos(angles), np.sin(angles)
    cos_tab = np.concatenate([cos, cos, cos, cos], axis=1)
    sin_tab = np.concatenate([-sin, sin, -sin, sin], axis=1)
    return jnp.asarray(cos_tab, F32), jnp.asarray(sin_tab, F32)


def swap_halves(vals):
    width = vals.shape[-1]
    lane = lax.broadcasted_iota(jnp.int32, vals.shape, 1)
    up = pltpu.roll(vals, width - HD // 2, 1)
    down = pltpu.roll(vals, HD // 2, 1)
    return jnp.where(lane % HD < HD // 2, up, down)


def widen(tab, width):
    reps = width // tab.shape[1]
    return tab if reps == 1 else jnp.concatenate([tab] * reps, axis=1)


def rope(vals, cos, sin):
    width = vals.shape[-1]
    return vals * widen(cos, width) + swap_halves(vals) * widen(sin, width)


def unrope(vals, cos, sin):
    width = vals.shape[-1]
    return vals * widen(cos, width) - swap_halves(vals) * widen(sin, width)


def params(semantics=None):
    return pltpu.CompilerParams(dimension_semantics=semantics, vmem_limit_bytes=VMEM_LIMIT)


def cost(micros):
    return pl.CostEstimate(flops=0, transcendentals=0, bytes_accessed=int(micros * COST * 3.69e6))


def project_kernel(pos_ref, x_ref, gain_ref, wq_ref, wk_ref, wv_ref, cos_ref, sin_ref, kv_ref, aux_ref):
    x = x_ref[...].astype(F32)
    inv = lax.rsqrt(jnp.mean(x * x, axis=-1, keepdims=True) + NORM_EPS)
    x1 = (x * inv * gain_ref[...]).astype(BF)
    cos, sin = cos_ref[...], sin_ref[...]
    q = rope(nn(x1, wq_ref[...]), cos, sin).astype(BF)
    q = (q.astype(F32) * (HD**-0.5)).astype(BF)
    k = rope(nn(x1, wk_ref[...]), cos, sin).astype(BF)
    v = nn(x1, wv_ref[...]).astype(BF)
    peers, _, rows, _ = aux_ref.shape
    aux = [q[:, m * LANES : (m + 1) * LANES] for m in range(q.shape[1] // LANES)]
    db = x.shape[1] // peers
    for p in range(peers):
        kv_ref[p, 0] = k
        kv_ref[p, 1] = v
        for m in range(len(aux)):
            aux_ref[p, m] = aux[m]
        cols = x1[:, p * db : (p + 1) * db]
        if db < LANES:
            cols = jnp.concatenate([cols, jnp.zeros((rows, LANES - db), BF)], axis=1)
        aux_ref[p, len(aux)] = cols


def project(pos, peers, block_in, gain, wq, wk, wv, cos, sin):
    rows, width = block_in.shape
    planes = wq.shape[1] // LANES + 1
    full = lambda shape: pl.BlockSpec(shape, lambda g, p: (0,) * len(shape))
    tab = pl.BlockSpec((rows, LANES), lambda g, p: (p[0], 0))
    return pl.pallas_call(
        project_kernel,
        grid_spec=pltpu.PrefetchScalarGridSpec(
            num_scalar_prefetch=1,
            grid=(1,),
            in_specs=[
                full((rows, width)),
                full((1, width)),
                full(wq.shape),
                full(wk.shape),
                full(wv.shape),
                tab,
                tab,
            ],
            out_specs=[full((peers, 2, rows, LANES)), full((peers, planes, rows, LANES))],
        ),
        out_shape=[
            jax.ShapeDtypeStruct((peers, 2, rows, LANES), BF),
            jax.ShapeDtypeStruct((peers, planes, rows, LANES), BF),
        ],
        compiler_params=params(),
        cost_estimate=cost(3),
        name="project",
    )(pos, block_in, gain, wq, wk, wv, cos, sin)


def attend_kernel(pos_ref, q_ref, kv_ref, out_ref):
    i = pos_ref[0]
    blocks, _, rows, kw = kv_ref.shape
    heads = kw // HD
    group = q_ref.shape[2] // HD
    n = blocks * rows
    k_all = kv_ref[:, 0].reshape(n, kw)
    v_all = kv_ref[:, 1].reshape(n, kw)
    col = lax.broadcasted_iota(jnp.int32, (group * rows, n), 1)
    row = lax.broadcasted_iota(jnp.int32, (group * rows, n), 0) % rows + i * rows
    allowed = col <= row
    for h in range(heads):
        k = k_all[:, h * HD : (h + 1) * HD]
        v = v_all[:, h * HD : (h + 1) * HD]
        q = jnp.concatenate([q_ref[h, :, g * HD : (g + 1) * HD] for g in range(group)], axis=0)
        s = jnp.where(allowed, nt(q, k), -1e30)
        top = jnp.max(s, axis=-1, keepdims=True)
        e = jnp.exp(s - top)
        total = jnp.sum(e, axis=-1, keepdims=True)
        o = (nn(e.astype(BF), v) / total).astype(BF)
        for g in range(group):
            c = (h * group + g) * HD
            out_ref[:, c : c + HD] = o[g * rows : (g + 1) * rows]


def attend(pos, aux, kv_all):
    _, _, rows, _ = aux.shape
    q_planes = kv_all.shape[3] // HD
    return pl.pallas_call(
        attend_kernel,
        grid_spec=pltpu.PrefetchScalarGridSpec(
            num_scalar_prefetch=1,
            grid=(1,),
            in_specs=[
                pl.BlockSpec((None, q_planes, rows, LANES), lambda g, p: (0, 0, 0, 0)),
                pl.BlockSpec(kv_all.shape, lambda g, p: (0, 0, 0, 0)),
            ],
            out_specs=pl.BlockSpec((rows, q_planes * LANES), lambda g, p: (0, 0)),
        ),
        out_shape=jax.ShapeDtypeStruct((rows, q_planes * LANES), BF),
        compiler_params=params(),
        cost_estimate=cost(3),
        name="attend",
    )(pos, aux, kv_all)


def mid_kernel(n_sh, *refs):
    pos_ref = refs[0]
    heads = refs[1 : n_sh + 1]
    ow = refs[n_sh + 1 : 2 * n_sh + 1]
    x_ref, gain_ref, router_ref, routes_ref, resid_ref, x2_ref, gates_ref, send_ref = refs[2 * n_sh + 1 :]
    acc = x_ref[...].astype(F32)
    for h, w in zip(heads, ow):
        acc = acc + nn(h[...], w[...])
    resid_ref[...] = acc
    inv = lax.rsqrt(jnp.mean(acc * acc, axis=-1, keepdims=True) + NORM_EPS)
    x2 = (acc * inv * gain_ref[...]).astype(BF)
    x2_ref[...] = x2
    logits = nn(x2, router_ref[...])
    lane = lax.broadcasted_iota(jnp.int32, logits.shape, 1)
    chosen = lane < 0
    for k in range(routes_ref.shape[1]):
        chosen = chosen | (routes_ref[:, k : k + 1] == lane)
    masked = jnp.where(chosen, logits, -1e30)
    e = jnp.where(chosen, jnp.exp(masked - jnp.max(masked, axis=-1, keepdims=True)), 0.0)
    gates = e / jnp.sum(e, axis=-1, keepdims=True)
    gates_ref[...] = gates
    rows, width = acc.shape
    planes = width // n_sh // LANES
    n_gate = send_ref.shape[1] - planes * rows
    g_rows = jnp.transpose(gates)[:n_gate].astype(BF)
    s = pos_ref[1]
    mine = []
    for m in range(planes):
        plane = x2[:, m * LANES : (m + 1) * LANES]
        for k in range(1, n_sh):
            at = (k * planes + m) * LANES
            plane = jnp.where(s == k, x2[:, at : at + LANES], plane)
        mine.append(plane)
    for m in range(planes):
        send_ref[0, m * rows : (m + 1) * rows] = mine[m]
    send_ref[0, planes * rows :] = g_rows


def mid(pos, n_gate, heads, ow, block_in, gain, router_pad, routes):
    rows, width = block_in.shape
    n_sh = len(heads)
    total = width // n_sh // LANES * rows + n_gate
    return pl.pallas_call(
        functools.partial(mid_kernel, n_sh),
        in_specs=[pl.BlockSpec(memory_space=pltpu.SMEM)] + [pl.BlockSpec()] * (2 * n_sh + 4),
        out_shape=[
            jax.ShapeDtypeStruct((rows, width), F32),
            jax.ShapeDtypeStruct((rows, width), BF),
            jax.ShapeDtypeStruct((rows, LANES), F32),
            jax.ShapeDtypeStruct((1, total, LANES), BF),
        ],
        compiler_params=params(),
        cost_estimate=cost(4),
        name="mid",
    )(pos, *heads, *ow, block_in, gain, router_pad, routes)


def expert_terms(pg, pu, g_out, gate):
    sig = 0.5 + 0.5 * jnp.tanh(0.5 * pg)
    silu = pg * sig
    hid = silu * pu
    dh = gate * g_out
    dpg = (dh * pu * (sig * (1.0 + pg * (1.0 - sig)))).astype(BF)
    dpu = (dh * silu).astype(BF)
    return hid, dpg, dpu


def experts_own_kernel(pos_ref, x_ref, og_ref, gates_ref, wg_ref, wu_ref, wd_ref, moe_ref, ex_ref, acc_m, acc_d, acc_g):
    e = pl.program_id(0)
    n_e = pl.num_programs(0)
    width = x_ref.shape[1]

    @pl.when(e == 0)
    def _():
        acc_m[...] = jnp.zeros_like(acc_m)
        acc_d[...] = jnp.zeros_like(acc_d)
        acc_g[...] = jnp.zeros_like(acc_g)

    lane = lax.broadcasted_iota(jnp.int32, gates_ref.shape, 1)
    mine = lane == pos_ref[1] * n_e + e
    gate = jnp.sum(jnp.where(mine, gates_ref[...], 0.0), axis=-1, keepdims=True)
    x = x_ref[...]
    wg, wu, wd = wg_ref[0], wu_ref[0], wd_ref[0]
    pg, pu, g_out = nn(x, wg), nn(x, wu), nt(og_ref[...].astype(BF), wd)
    hid, dpg, dpu = expert_terms(pg, pu, g_out, gate)
    d_gate = jnp.sum(hid.astype(BF).astype(F32) * g_out, axis=-1, keepdims=True)
    acc_m[...] += nn((gate * hid).astype(BF), wd)
    acc_d[...] += nt(dpg, wg) + nt(dpu, wu)
    acc_g[...] += jnp.where(mine, d_gate, 0.0)

    @pl.when(e == n_e - 1)
    def _():
        moe_ref[...] = acc_m[...].astype(BF)
        ex_ref[:, :width] = acc_d[...].astype(BF)
        ex_ref[:, width:] = acc_g[...].astype(BF)


def experts_own(pos, x2, og, gates, wg, wu, wd):
    rows, width = x2.shape
    n_e, _, ff = wg.shape
    full = lambda shape: pl.BlockSpec(shape, lambda e, p: (0,) * len(shape))
    return pl.pallas_call(
        experts_own_kernel,
        grid_spec=pltpu.PrefetchScalarGridSpec(
            num_scalar_prefetch=1,
            grid=(n_e,),
            in_specs=[
                full((rows, width)),
                full((rows, width)),
                full((rows, LANES)),
                pl.BlockSpec((1, width, ff), lambda e, p: (e, 0, 0)),
                pl.BlockSpec((1, width, ff), lambda e, p: (e, 0, 0)),
                pl.BlockSpec((1, ff, width), lambda e, p: (e, 0, 0)),
            ],
            out_specs=[full((rows, width)), full((rows, width + LANES))],
            scratch_shapes=[
                pltpu.VMEM((rows, width), F32),
                pltpu.VMEM((rows, width), F32),
                pltpu.VMEM((rows, LANES), F32),
            ],
        ),
        out_shape=[
            jax.ShapeDtypeStruct((rows, width), BF),
            jax.ShapeDtypeStruct((rows, width + LANES), BF),
        ],
        compiler_params=params(("arbitrary",)),
        cost_estimate=cost(11),
        name="experts_own",
    )(pos, x2, og, gates, wg, wu, wd)


def back_mid_kernel(
    n_exp, ex_ref, far_ref, resid_ref, gain_ref, gates_ref, router_ref, og_ref, ow_ref, dmid_ref, send_ref
):
    rows, width = resid_ref.shape
    ex = ex_ref[...].astype(F32) + far_ref[...].astype(F32)
    gates = gates_ref[...]
    d_gate = ex[:, width:]
    d_logits = gates * (d_gate - jnp.sum(gates * d_gate, axis=-1, keepdims=True))
    d_norm = ex[:, :width] + nt(d_logits.astype(BF), router_ref[...])
    resid = resid_ref[...]
    inv = lax.rsqrt(jnp.mean(resid * resid, axis=-1, keepdims=True) + NORM_EPS)
    hat = resid * inv
    d_gain = jnp.sum(d_norm * hat, axis=0, keepdims=True)
    u = gain_ref[...] * d_norm
    inner = jnp.mean(u * hat, axis=-1, keepdims=True)
    d_mid = og_ref[...] + inv * (u - hat * inner)
    dmid_ref[...] = d_mid
    dmb = d_mid.astype(BF)
    d_heads = nt(dmb, ow_ref[...]).astype(BF)
    planes = d_heads.shape[1] // LANES
    gain_rows = [d_gain[:, k * LANES : (k + 1) * LANES] for k in range(width // LANES)]
    small = jnp.concatenate([jnp.transpose(d_logits)[:n_exp]] + gain_rows, axis=0).astype(BF)
    peers = send_ref.shape[0]
    db = width // peers
    for p in range(peers):
        for m in range(planes):
            send_ref[p, m * rows : (m + 1) * rows] = d_heads[:, m * LANES : (m + 1) * LANES]
        cols = dmb[:, p * db : (p + 1) * db]
        if db < LANES:
            cols = jnp.concatenate([cols, jnp.zeros((rows, LANES - db), BF)], axis=1)
        send_ref[p, planes * rows : (planes + 1) * rows] = cols
        send_ref[p, (planes + 1) * rows :] = small


def back_mid(peers, n_exp, ex, far, resid, gain, gates, router_pad, og, ow):
    rows, width = resid.shape
    total = (ow.shape[0] // LANES + 1) * rows + n_exp + width // LANES
    return pl.pallas_call(
        functools.partial(back_mid_kernel, n_exp),
        out_shape=[
            jax.ShapeDtypeStruct((rows, width), F32),
            jax.ShapeDtypeStruct((peers, total, LANES), BF),
        ],
        compiler_params=params(),
        cost_estimate=cost(3),
        name="back_mid",
    )(ex, far, resid, gain, gates, router_pad, og, ow)


def block_probs(q, k, start, first, bq):
    s = nt(q, k)
    edge = s[:, first:]
    col = lax.broadcasted_iota(jnp.int32, edge.shape, 1) + first
    row = lax.broadcasted_iota(jnp.int32, edge.shape, 0) % bq + start
    edge = jnp.where(col <= row, edge, -1e30)
    s = edge if first == 0 else jnp.concatenate([s[:, :first], edge], axis=1)
    e = jnp.exp(s - jnp.max(s, axis=-1, keepdims=True))
    return e, 1.0 / jnp.sum(e, axis=-1, keepdims=True)


def load_heads(dst, block, j, h):
    rows = block.shape[0]
    for g in range(LANES // HD):
        dst[h, g, j * rows : (j + 1) * rows] = block[:, g * HD : (g + 1) * HD]


def load_keys(ks, vs, kv_ref):
    blocks, _, rows, kw = kv_ref.shape
    for j in range(blocks):
        for h in range(kw // HD):
            ks[h, j * rows : (j + 1) * rows] = kv_ref[j, 0, :, h * HD : (h + 1) * HD]
            vs[h, j * rows : (j + 1) * rows] = kv_ref[j, 1, :, h * HD : (h + 1) * HD]


def stacked(src, h, start, bq):
    return jnp.concatenate([src[h, g, pl.ds(start, bq)] for g in range(LANES // HD)], axis=0)


def attend_back_kernel(n_exp, *refs):
    pos_ref, q_ref, kv_ref, do_ref, cos_ref, sin_ref, wq_ref, wk_ref, wv_ref, gcol_ref, moe_ref = refs[:11]
    dn_ref, qg_ref, kg_ref, vg_ref, og_ref, mg_ref, qs, ks, vs, dos, dqs, dkt, dvt, dqkv, hos, hfull = refs[11:]
    i = pos_ref[0]
    blocks, _, rows, kw = kv_ref.shape
    heads = kw // HD
    group = LANES // HD
    qw = heads * LANES
    n = blocks * rows
    bq = 4 * rows if n <= 1024 else rows // 2
    load_keys(ks, vs, kv_ref)
    for j in range(blocks):
        for h in range(heads):
            load_heads(qs, q_ref[j, h], j, h)
            load_heads(dos, do_ref[j, h * rows : (h + 1) * rows], j, h)
    dkt[...] = jnp.zeros_like(dkt)
    dvt[...] = jnp.zeros_like(dvt)

    def step(h, start, ext, first):
        k, v = ks[h, :ext], vs[h, :ext]
        q, do = stacked(qs, h, start, bq), stacked(dos, h, start, bq)
        e, inv = block_probs(q, k, start, first, bq)
        p = e * inv
        pb = p.astype(BF)
        o = nn(pb, v).astype(BF)
        delta = jnp.sum(do.astype(F32) * o.astype(F32), axis=-1, keepdims=True)
        ds = (p * (nt(do, v) - delta)).astype(BF)
        dq = nn(ds, k) * (HD**-0.5)
        dkt[h, :, :ext] += tn(q, ds)
        dvt[h, :, :ext] += tn(do, pb)
        for g in range(group):
            dqs[h, g, pl.ds(start, bq)] = dq[g * bq : (g + 1) * bq]
            hos[h, g, pl.ds(start, bq)] = o[g * bq : (g + 1) * bq]

    def per_head(h, carry):
        if n <= 1024:
            for r in range(n // bq):
                step(h, r * bq, (r + 1) * bq, r * bq)
        else:

            def loop(r, c):
                step(h, pl.multiple_of(r * bq, bq), n, 0)
                return c

            lax.fori_loop(0, n // bq, loop, 0)
        return carry

    lax.fori_loop(0, heads, per_head, 0, unroll=n <= 1024)
    pieces = [(h, g) for h in range(heads) for g in range(group)]
    small = (heads + 1) * rows
    gain_rows = jnp.sum(do_ref[:, small + n_exp :].astype(F32), axis=0)
    mine = lax.broadcasted_iota(jnp.int32, gain_rows.shape, 0) == pos_ref[2]
    mg_ref[...] = jnp.sum(jnp.where(mine, gain_rows, 0.0), axis=0, keepdims=True)

    def per_block(j, carry):
        at = pl.ds(pl.multiple_of(j * rows, rows), rows)
        cos, sin = cos_ref[at], sin_ref[at]
        hfull[at] = jnp.concatenate([hos[h, g, at] for h, g in pieces], axis=1)
        dq = jnp.concatenate([dqs[h, g, at] for h, g in pieces], axis=1)
        dk = jnp.transpose(jnp.concatenate([dkt[h, :, at] for h in range(heads)], axis=0))
        dv = jnp.transpose(jnp.concatenate([dvt[h, :, at] for h in range(heads)], axis=0))
        out = jnp.concatenate([unrope(dq, cos, sin), unrope(dk, cos, sin), dv], axis=1).astype(BF)
        dqkv[j] = out
        return carry

    lax.fori_loop(0, blocks, per_block, 0, unroll=2)
    qkvg = tn(q_ref[:, q_ref.shape[1] - 1].reshape(n, LANES), dqkv[...].reshape(n, qw + 2 * kw))
    qg_ref[...] = qkvg[:, :qw]
    kg_ref[...] = qkvg[:, qw : qw + kw]
    vg_ref[...] = qkvg[:, qw + kw :]
    og_ref[...] = tn(hfull[...], do_ref[:, heads * rows : (heads + 1) * rows].reshape(n, LANES))
    own = dqkv[i]
    width = wq_ref.shape[0]
    db = width // blocks
    dn_ref[:, :width] = (
        nt(own[:, :qw], wq_ref[...]) + nt(own[:, qw : qw + kw], wk_ref[...]) + nt(own[:, qw + kw :], wv_ref[...])
    ).astype(BF)
    mine = pl.ds(pl.multiple_of(i * db, db), db)
    w_rows = jnp.concatenate([wq_ref[mine], wk_ref[mine], wv_ref[mine]], axis=1).astype(F32)
    gain = jnp.sum(qkvg[:db] * w_rows, axis=1, keepdims=True) / gcol_ref[mine]
    if db < rows:
        gain = jnp.concatenate([gain, jnp.zeros((rows - db, 1), F32)], axis=0)
    dn_ref[:, width : width + LANES] = jnp.broadcast_to(gain, (rows, LANES)).astype(BF)
    dn_ref[:, width + LANES :] = moe_ref[...]


def attend_back(n_exp, pos, q_all, kv_all, do_all, cos, sin, wq, wk, wv, gain_col, moe):
    blocks, _, rows, kw = kv_all.shape
    width, qw = wq.shape
    heads, group = kw // HD, LANES // HD
    n = blocks * rows
    per_head = pltpu.VMEM((heads, group, n, HD), BF)
    return pl.pallas_call(
        functools.partial(attend_back_kernel, n_exp),
        in_specs=[pl.BlockSpec(memory_space=pltpu.SMEM)] + [pl.BlockSpec()] * 10,
        out_shape=[
            jax.ShapeDtypeStruct((rows, 2 * width + LANES), BF),
            jax.ShapeDtypeStruct((LANES, qw), F32),
            jax.ShapeDtypeStruct((LANES, kw), F32),
            jax.ShapeDtypeStruct((LANES, kw), F32),
            jax.ShapeDtypeStruct((qw, LANES), F32),
            jax.ShapeDtypeStruct((1, LANES), F32),
        ],
        scratch_shapes=[
            per_head,
            pltpu.VMEM((heads, n, HD), BF),
            pltpu.VMEM((heads, n, HD), BF),
            per_head,
            pltpu.VMEM((heads, group, n, HD), F32),
            pltpu.VMEM((heads, HD, n), F32),
            pltpu.VMEM((heads, HD, n), F32),
            pltpu.VMEM((blocks, rows, qw + 2 * kw), BF),
            per_head,
            pltpu.VMEM((n, qw), BF),
        ],
        compiler_params=params(),
        cost_estimate=cost(18),
        name="attend_back",
    )(pos, q_all, kv_all, do_all, cos, sin, wq, wk, wv, gain_col, moe)


def experts_all_kernel(n_sh, rows, n_exp, *refs):
    pos_ref, refs = refs[0], refs[1:]
    xs, ogs = refs[:n_sh], refs[n_sh : 2 * n_sh]
    small_ref = refs[2 * n_sh]
    base = 2 * n_sh + 1
    wgs, wus, wds = (refs[base + k * n_sh : base + (k + 1) * n_sh] for k in range(3))
    gg_ref, ug_ref, dg_ref, rg_ref, acc = refs[base + 3 * n_sh :]
    e, c = pl.program_id(0), pl.program_id(1)
    nb = xs[0].shape[0]
    tb = nb * rows
    planes = wgs[0].shape[1] // LANES
    lane = lax.broadcasted_iota(jnp.int32, (tb, LANES), 1)
    mine = lane == pos_ref[1] * pl.num_programs(0) + e
    pad = jnp.zeros((LANES - n_exp, rows), F32)
    gates = [jnp.transpose(jnp.concatenate([xs[0][t, planes * rows :].astype(F32), pad], axis=0)) for t in range(nb)]
    gate = jnp.sum(jnp.where(mine, jnp.concatenate(gates, axis=0), 0.0), axis=-1, keepdims=True)
    x_planes = [[x[:, m * rows : (m + 1) * rows].reshape(tb, LANES) for m in range(planes)] for x in xs]
    block = [pos_ref[3 + c * nb + t] for t in range(nb)]
    o_planes = [[o[:, m].reshape(tb, LANES) for m in range(planes)] for o in ogs]
    xv = [jnp.concatenate(p, axis=1) for p in x_planes]
    ov = [jnp.concatenate(p, axis=1) for p in o_planes]
    pg = sum(nn(x, w[0]) for x, w in zip(xv, wgs))
    pu = sum(nn(x, w[0]) for x, w in zip(xv, wus))
    g_out = sum(nt(o, w[0]) for o, w in zip(ov, wds))
    hid, dpg, dpu = expert_terms(pg, pu, g_out, gate)
    hg = (gate * hid).astype(BF)
    plane = pos_ref[2]
    xc, oc = x_planes[0][0], o_planes[0][0]
    for b in range(n_sh):
        for m in range(planes):
            hit = plane == (pos_ref[1] ^ b) * planes + m
            xc = jnp.where(hit, x_planes[b][m], xc)
            oc = jnp.where(hit, o_planes[b][m], oc)

    @pl.when(e == 0)
    def _():
        part = nn(jnp.concatenate([small_ref[j, :n_exp] for j in block], axis=1), xc)

        @pl.when(c == 0)
        def _():
            rg_ref[...] = part

        @pl.when(c > 0)
        def _():
            rg_ref[...] += part

    gg, ug, dg = tn(xc, dpg), tn(xc, dpu), tn(oc, hg)

    @pl.when(c == 0)
    def _():
        gg_ref[0] = gg
        ug_ref[0] = ug
        acc[...] = dg

    @pl.when(c > 0)
    def _():
        gg_ref[0] += gg
        ug_ref[0] += ug
        acc[...] += dg

    @pl.when(c == pl.num_programs(1) - 1)
    def _():
        dg_ref[0] = jnp.transpose(acc[...])


def experts_all(n_exp, pos, xs, ogs, small, wg, wu, wd):
    n_sh = len(xs)
    blocks, total, _ = xs[0].shape
    _, planes, rows, _ = ogs[0].shape
    piece = planes * LANES
    n = blocks * rows
    n_e, width, ff = wg.shape
    nb = math.gcd(blocks, 8)
    tail = small.shape[1] % rows
    x_tok = pl.BlockSpec((nb, total, LANES), lambda e, c, p: (c, 0, 0))
    o_tok = pl.BlockSpec((nb, planes, rows, LANES), lambda e, c, p: (c, 0, 0, 0))
    row_w = lambda b: pl.BlockSpec((1, piece, ff), lambda e, c, p, b=b: (e, p[1] ^ b, 0))
    col_w = lambda b: pl.BlockSpec((1, ff, piece), lambda e, c, p, b=b: (e, 0, p[1] ^ b))
    out = pl.BlockSpec((1, LANES, ff), lambda e, c, p: (e, 0, 0))
    out_t = pl.BlockSpec((1, ff, LANES), lambda e, c, p: (e, 0, 0))
    sh = range(n_sh)
    return pl.pallas_call(
        functools.partial(experts_all_kernel, n_sh, rows, n_exp),
        grid_spec=pltpu.PrefetchScalarGridSpec(
            num_scalar_prefetch=1,
            grid=(n_e, blocks // nb),
            in_specs=[x_tok for _ in sh]
            + [o_tok for _ in sh]
            + [pl.BlockSpec((blocks, tail, LANES), lambda e, c, p: (0, small.shape[1] // tail - 1, 0))]
            + [row_w(b) for b in sh]
            + [row_w(b) for b in sh]
            + [col_w(b) for b in sh],
            out_specs=[out, out, out_t, pl.BlockSpec((n_exp, LANES), lambda e, c, p: (0, 0))],
            scratch_shapes=[pltpu.VMEM((LANES, ff), F32)],
        ),
        out_shape=[jax.ShapeDtypeStruct((n_e, LANES, ff), F32)] * 2
        + [jax.ShapeDtypeStruct((n_e, ff, LANES), F32), jax.ShapeDtypeStruct((n_exp, LANES), F32)],
        compiler_params=params(("arbitrary", "arbitrary")),
        cost_estimate=cost(25),
        name="experts_all",
    )(pos, *xs, *ogs, small, *[wg] * n_sh, *[wu] * n_sh, *[wd] * n_sh)


def finish_kernel(near_ref, far_ref, x_ref, gain_ref, dmid_ref, resid_ref, out_ref, dgain_ref, block_ref):
    width = x_ref.shape[1]
    total = near_ref[...].astype(F32) + far_ref[...].astype(F32)
    block_ref[...] = resid_ref[...] + total[:, width + LANES :]
    dgain_ref[...] = jnp.transpose(total[:, width : width + LANES])[:1]
    x = x_ref[...].astype(F32)
    inv = lax.rsqrt(jnp.mean(x * x, axis=-1, keepdims=True) + NORM_EPS)
    hat = x * inv
    u = gain_ref[...] * total[:, :width]
    out_ref[...] = dmid_ref[...] + inv * (u - hat * jnp.mean(u * hat, axis=-1, keepdims=True))


def finish(near, far, block_in, gain, d_mid, resid):
    rows, width = block_in.shape
    return pl.pallas_call(
        finish_kernel,
        out_shape=[
            jax.ShapeDtypeStruct((rows, width), F32),
            jax.ShapeDtypeStruct((1, rows), F32),
            jax.ShapeDtypeStruct((rows, width), F32),
        ],
        compiler_params=params(),
        cost_estimate=cost(2),
        name="finish",
    )(near, far, block_in, gain, d_mid, resid)


def exchange(x, bit):
    size = lax.axis_size("shard")
    return lax.ppermute(x, "shard", [(j, j ^ bit) for j in range(size)])


def double_ctx(x, bit):
    size = lax.axis_size("ctx")
    far = lax.ppermute(x, "ctx", [(j, j ^ bit) for j in range(size)])
    return jnp.concatenate([x, far], axis=0)


def ctx_bits():
    count = lax.axis_size("ctx").bit_length() - 1
    return [1 << b for b in reversed(range(count))]


def ctx_order(size):
    order = [0]
    bit = size // 2
    while bit:
        order = order + [o ^ bit for o in order]
        bit //= 2
    return jnp.array(order, jnp.int32) ^ lax.axis_index("ctx")


def swap_ctx(x):
    return lax.all_to_all(x, "ctx", 0, 0, tiled=True)


def gather_shard(x):
    found = {0: x}
    bit = lax.axis_size("shard") // 2
    while bit:
        for off in list(found):
            found[off ^ bit] = exchange(found[off], bit)
        bit //= 2
    return [found[b] for b in range(len(found))]


def halves_shard(x):
    last = lax.axis_size("shard") // 2
    bit = 1
    while bit < last:
        x = (x.astype(F32) + exchange(x, bit).astype(F32)).astype(x.dtype)
        bit *= 2
    return x, exchange(x, last)


def after(x, token):
    return lax.optimization_barrier((x, token))[0]


def body(
    block_in,
    attn_gain,
    q_weight,
    k_weight,
    v_weight,
    o_weight,
    moe_gain,
    router_weight,
    expert_gate,
    expert_up,
    expert_down,
    routes,
    out_grad,
):
    rows, width = block_in.shape
    n_ctx, n_sh = lax.axis_size("ctx"), lax.axis_size("shard")
    seq_len = rows * n_ctx
    n_exp = router_weight.shape[1]
    db = width // n_ctx
    qw, kw = q_weight.shape[1], k_weight.shape[1]
    q_planes = qw // LANES
    i, s = lax.axis_index("ctx"), lax.axis_index("shard")
    lane_at = (i * db) % LANES
    pos = jnp.concatenate([jnp.stack([i, s, (i * db) // LANES]).astype(jnp.int32), ctx_order(n_ctx)])
    cos, sin = rope_constants(seq_len)
    gain_one = attn_gain.reshape(1, width)
    gain_two = moe_gain.reshape(1, width)
    router_pad = jnp.pad(router_weight, ((0, 0), (0, LANES - n_exp)))

    piece = width // n_sh
    bits = ctx_bits()
    og_all = lax.dynamic_slice_in_dim(out_grad, s * piece, piece, 1).astype(BF)
    og_all = og_all.reshape(1, rows, piece // LANES, LANES).swapaxes(1, 2)
    og_all = double_ctx(og_all, bits[0])
    kv_send, aux_send = project(
        pos, n_ctx, block_in, gain_one, q_weight, k_weight, v_weight, cos, sin
    )
    kv_all = swap_ctx(kv_send)
    ow = gather_shard(o_weight)
    kv_all = after(kv_all, (ow, og_all))
    for bit in bits[1:-1]:
        og_all = double_ctx(og_all, bit)
    aux_all = swap_ctx(after(aux_send, kv_all))
    heads = attend(pos, aux_send, kv_all)
    resid_mid, x2, gates, x2_send = mid(
        pos, n_exp, gather_shard(heads), ow, block_in, gain_two, router_pad, routes
    )
    x2 = after(x2, og_all)
    og_all = double_ctx(og_all, bits[-1])
    x2_all = double_ctx(x2_send, bits[0])
    moe_part, ex_part = experts_own(pos, x2, out_grad, gates, expert_gate, expert_up, expert_down)
    near, far = halves_shard(ex_part)
    x2_all = after(x2_all, near)
    for bit in bits[1:-1]:
        x2_all = double_ctx(x2_all, bit)
    d_mid, back_send = back_mid(
        n_ctx, n_exp, near, after(far, (x2_all, og_all)), resid_mid, gain_two, gates, router_pad, out_grad, o_weight
    )
    x2_all = double_ctx(x2_all, bits[-1])
    back_all = swap_ctx(after(back_send, aux_all))
    ogs = gather_shard(og_all)
    xs = gather_shard(x2_all)
    back_all = after(back_all, (ogs[n_sh // 2], x2_all))
    dn_part, q_grad, k_grad, v_grad, o_grad, moe_gain_sum = attend_back(
        n_exp, pos, aux_all, kv_all, back_all, cos, sin, q_weight, k_weight, v_weight,
        attn_gain.reshape(width, 1), moe_part
    )
    in_grad, gain_sum, block_out = finish(*halves_shard(dn_part), block_in, gain_one, d_mid, resid_mid)
    attn_gain_grad = gain_sum.reshape(rows)[:db]
    q_grad, k_grad, v_grad = q_grad[:db], k_grad[:db], v_grad[:db]
    o_grad = o_grad[:, :db]

    gate_grad, up_grad, down_grad, router_t = experts_all(
        n_exp, pos, xs, ogs, back_all, expert_gate, expert_up, expert_down
    )
    if db < LANES:
        gate_grad = lax.dynamic_slice_in_dim(gate_grad, lane_at, db, 1)
        up_grad = lax.dynamic_slice_in_dim(up_grad, lane_at, db, 1)
        down_grad = lax.dynamic_slice_in_dim(down_grad, lane_at, db, 2)
        router_t = lax.dynamic_slice_in_dim(router_t, lane_at, db, 1)
    router_grad = router_t.T
    moe_gain_grad = moe_gain_sum.reshape(LANES)
    if db < LANES:
        moe_gain_grad = lax.dynamic_slice_in_dim(moe_gain_grad, lane_at, db, 0)
    return (
        block_out,
        in_grad,
        attn_gain_grad,
        q_grad,
        k_grad,
        v_grad,
        o_grad,
        moe_gain_grad,
        router_grad,
        gate_grad,
        up_grad,
        down_grad,
    )


def solution(mesh):
    in_specs = (
        P("ctx", None),
        P(),
        P(None, "shard"),
        P(None, "shard"),
        P(None, "shard"),
        P("shard", None),
        P(),
        P(),
        P("shard", None, None),
        P("shard", None, None),
        P("shard", None, None),
        P("ctx", None),
        P("ctx", None),
    )
    out_specs = (
        P("ctx", None),
        P("ctx", None),
        P("ctx"),
        P("ctx", "shard"),
        P("ctx", "shard"),
        P("ctx", "shard"),
        P("shard", "ctx"),
        P("ctx"),
        P("ctx", None),
        P("shard", "ctx", None),
        P("shard", "ctx", None),
        P("shard", None, "ctx"),
    )
    return jax.shard_map(body, mesh=mesh, in_specs=in_specs, out_specs=out_specs, check_vma=False)
```
